256 devices in a mesh: grp: 16 (over y, z_lo, core), orb: 16 (over x, z_hi).
Axes of the slice: x: 4, y: 4, z: 8 (z_hi: 4, z_lo: 2; z = z_hi * 2 + z_lo), core: 2. Of those that a mesh axis runs over, the one named last changes fastest.
Arguments:
- slabs: float32 [256, 256, 1024], P(('grp', 'orb')), may hold values from -0.9 to 0.9
- eps_occ: float32 [256], P(('grp', 'orb')), may hold values from -1.5 to -0.5
- eps_vir: float32 [256], replicated, may hold values from 0.2 to 3
Outputs:
- gradient: float32 [256, 256, 1024], P(('grp', 'orb'))
- density: float32 [256, 256], P('orb')
The draws below stay inside these ranges and needn't reach their ends.
All inputs are finite; a program needn't handle non-finite values.
Results may differ from the reference program's by a relative error of at most 0.0003.
Values sent between devices are 32-bit elements; how exact they have to be, the bound alone decides.
No kernel may reach another device: no remote copies, remote signals or barrier semaphores. Data moves between devices by JAX's collectives and lax.ppermute only.
A program may use at most 64 MiB of HBM per device.

```python
import jax
import jax.numpy as jnp
from jax import lax

V = 256
NAUX = 1024
NOCC = 256


def levels(rng, extent, pieces, smallest, largest):
    factor_of, own = 1.0, jax.random.fold_in(rng, 6)
    for axis_at, shards_of in pieces:
        heights = jnp.exp(jax.random.uniform(jax.random.fold_in(own, axis_at), (shards_of,), jnp.float32, smallest / len(pieces), largest / len(pieces)))
        factor_of = factor_of * jnp.repeat(heights, extent[axis_at] // shards_of).reshape([-1 if axis == axis_at else 1 for axis in range(len(extent))])
    return factor_of


def scatter_about(rng, shape, spread, limit, cuts=(), kind=jnp.bfloat16):
    result = spread * jax.random.normal(rng, shape, jnp.float32)
    if cuts:
        result = result * levels(rng, shape, cuts, -0.22, 0.18)
    return jnp.clip(result, -limit, limit).astype(kind)


def setup_inputs(seed: int = 0) -> dict:
    key_list = jax.random.split(jax.random.key(seed), 4)
    slabs = scatter_about(key_list[0], (NOCC, V, NAUX), 0.15, 0.9, ((0, 256),), jnp.float32)
    eps_occ = jnp.clip(-1.5 + 1.0 * jax.random.uniform(key_list[1], (NOCC,), jnp.float32) ** levels(key_list[1], (NOCC,), ((0, 256),), -0.2, 0.2), -1.5, -0.5)
    eps_vir = jnp.clip(jax.random.uniform(key_list[2], (V,), jnp.float32, 0.2, 3.0), 0.2, 3.0)
    return {"slabs": slabs, "eps_occ": eps_occ, "eps_vir": eps_vir}


def pair_terms(own, other, e_own, e_other, eps_vir):
    coulomb = jnp.dot(own, other.T, precision=lax.Precision.HIGHEST, preferred_element_type=jnp.float32)
    denom = e_own + e_other - eps_vir[:, None] - eps_vir[None, :]
    amps = coulomb / denom
    spin = 2.0 * amps - amps.T
    grad = jnp.dot(spin, other, precision=lax.Precision.HIGHEST, preferred_element_type=jnp.float32)
    dens = jnp.dot(amps, spin.T, precision=lax.Precision.HIGHEST, preferred_element_type=jnp.float32)
    return grad, dens


def reference(slabs, eps_occ, eps_vir):
    def step(carry, index):
        own = slabs[index]
        grad = jnp.zeros((V, NAUX), jnp.float32)
        dens = carry
        for mask in (1, 2, 3):
            partner = jnp.bitwise_xor(index, jnp.int32(mask)).astype(jnp.int32)
            other = slabs[partner]
            g_part, d_part = pair_terms(own, other, eps_occ[index], eps_occ[partner], eps_vir)
            grad = grad + g_part
            dens = dens + d_part
        return dens, grad

    start = jnp.zeros((V, V), jnp.float32)
    dens, grads = lax.scan(step, start, jnp.arange(NOCC, dtype=jnp.int32))
    return grads, dens / NOCC
```

```python
import jax
import jax.numpy as jnp
from jax import lax
from jax.sharding import PartitionSpec as P

RING = 4
PREC = lax.Precision.HIGH


def shift(value, step):
    size = lax.axis_size("orb")
    pairs = [
        (at, at // RING * RING + (at % RING + step) % RING) for at in range(size)
    ]
    return lax.ppermute(value, "orb", pairs)


def mm(a, b, dims):
    return lax.dot_general(
        a, b, (dims, ((), ())), precision=PREC, preferred_element_type=jnp.float32
    )


def amplitudes(left, right, energy, eps_vir):
    coulomb = mm(left, right, ((1,), (1,)))
    amps = coulomb / (energy - eps_vir[:, None] - eps_vir[None, :])
    return amps, 2.0 * amps - amps.T


def per_device(slabs, eps_occ, eps_vir):
    own = slabs[0]
    half = own.shape[0] // 2
    own_a, own_b = own[:half], own[half:]
    low_a = shift(own_a, 1)
    high_b = shift(own_b, -1)
    low_b = shift(own_b, 1)
    high_a = shift(own_a, -1)
    far_a = shift(low_a, 1)
    far_b = shift(high_b, -1)
    e_low = shift(eps_occ, 1)
    e_high = shift(eps_occ, -1)
    e_far = shift(eps_occ, 2)

    low = jnp.concatenate([low_a, low_b], axis=0)
    high = jnp.concatenate([high_a, high_b], axis=0)
    far = jnp.concatenate([far_a, far_b], axis=0)
    t_low, s_low = amplitudes(own, low, eps_occ[0] + e_low[0], eps_vir)
    t_high, s_high = amplitudes(own, high, eps_occ[0] + e_high[0], eps_vir)
    t_mid, s_mid = amplitudes(low, high, e_low[0] + e_high[0], eps_vir)
    dens = mm(t_low, s_low, ((1,), (1,)))
    dens = dens + mm(t_high, s_high, ((1,), (1,)))
    dens = dens + mm(t_mid, s_mid, ((1,), (1,)))

    n_orb, n_grp = lax.axis_size("orb"), lax.axis_size("grp")
    rows = own.shape[0] // n_orb
    pieces = lax.all_to_all(
        dens.reshape(n_orb, rows, -1), "orb", split_axis=0, concat_axis=0, tiled=True
    )
    share = jnp.sum(pieces, axis=0) * (1.0 / (n_orb * n_grp))
    copies = lax.all_to_all(
        jnp.broadcast_to(share[None], (n_grp,) + share.shape),
        "grp",
        split_axis=0,
        concat_axis=0,
        tiled=True,
    )
    density = jnp.sum(copies, axis=0)

    grad = mm(s_low, low, ((1,), (0,))) + mm(s_high, high, ((1,), (0,)))
    _, s_far = amplitudes(own, far, eps_occ[0] + e_far[0], eps_vir)
    grad = grad + mm(s_far, far, ((1,), (0,)))
    return grad[None], density


def solution(mesh):
    placed = (P(("grp", "orb"), None, None), P(("grp", "orb")), P())
    return jax.shard_map(
        per_device,
        mesh=mesh,
        in_specs=placed,
        out_specs=(P(("grp", "orb"), None, None), P("orb", None)),
        check_vma=False,
    )
```

```python
import jax
import jax.numpy as jnp
from jax import lax
from jax.experimental import pallas as pl
from jax.experimental.pallas import tpu as pltpu
from jax.sharding import PartitionSpec as P


RING = 4
CUTS = (0, 32, 128, 224, 256)
VMEM = pl.BlockSpec(memory_space=pltpu.VMEM)
SMEM = pl.BlockSpec(memory_space=pltpu.SMEM)
F32, BF16 = jnp.float32, jnp.bfloat16


def shift(value, step):
    size = lax.axis_size("orb")
    pairs = [
        (at, at // RING * RING + (at % RING + step) % RING) for at in range(size)
    ]
    return lax.ppermute(value, "orb", pairs)


def split(x):
    high = x.astype(BF16)
    return high, (x - high.astype(F32)).astype(BF16)


def mm(a, b, contract):
    dims = ((contract, ((), ())))
    dot = lambda p, q: lax.dot_general(p, q, dims, preferred_element_type=F32)
    return dot(a[0], b[0]) + (dot(a[0], b[1]) + dot(a[1], b[0]))


ROWS = ((1,), (1,))
PLAIN = ((1,), (0,))


def fill(chunks, high, low):
    for at, chunk in enumerate(chunks):
        h, l = split(chunk[...])
        high[CUTS[at] : CUTS[at + 1], :] = h
        low[CUTS[at] : CUTS[at + 1], :] = l


def density_kernel(core, own, *refs):
    lows, highs, (r_low, r_high, r_mid) = refs[:4], refs[4:8], refs[8:11]
    keep, send, s_low, s_high = refs[11:15]
    oh, ol, lh, ll, hh, hl, dens = refs[15:]
    fill((own.at[a:b] for a, b in zip(CUTS[:-1], CUTS[1:])), oh, ol)
    fill(lows, lh, ll)
    fill(highs, hh, hl)
    o, l, h = (oh[...], ol[...]), (lh[...], ll[...]), (hh[...], hl[...])

    def term(left, right, recip):
        t = mm(left, right, ROWS) * recip[...]
        s = 2.0 * t - t.T
        return mm(split(t), split(s), ROWS), s

    total, s_low[...] = term(o, l, r_low)
    part, s_high[...] = term(o, h, r_high)
    total = total + part
    part, _ = term(l, h, r_mid)
    dens[...] = total + part
    mine = core[0] * 8
    for at in range(16):
        keep[at] = dens[pl.ds(pl.multiple_of(at * 16 + mine, 8), 8), :]
        send[at] = dens[pl.ds(pl.multiple_of(at * 16 + 8 - mine, 8), 8), :]


def near_kernel(*refs):
    lows, highs, (s_low, s_high, grad, lh, ll, hh, hl) = refs[:4], refs[4:8], refs[8:]
    fill(lows, lh, ll)
    fill(highs, hh, hl)
    grad[...] = mm(split(s_low[...]), (lh[...], ll[...]), PLAIN) + mm(
        split(s_high[...]), (hh[...], hl[...]), PLAIN
    )


def far_kernel(own, *refs):
    fars, (recip, near, grad, oh, ol, fh, fl) = refs[:4], refs[4:]
    fill((own.at[a:b] for a, b in zip(CUTS[:-1], CUTS[1:])), oh, ol)
    fill(fars, fh, fl)
    f = (fh[...], fl[...])
    t = mm((oh[...], ol[...]), f, ROWS) * recip[...]
    s = 2.0 * t - t.T
    grad[...] = near[...] + mm(split(s), f, PLAIN)


def call(kernel, out, n_split, extra, flops, args, scalars=0):
    v, n = 256, 1024
    shapes = tuple(jax.ShapeDtypeStruct(s, F32) for s in out)
    return pl.pallas_call(
        kernel,
        out_shape=shapes,
        in_specs=[SMEM] * scalars + [VMEM] * (len(args) - scalars),
        out_specs=tuple(VMEM for _ in out),
        scratch_shapes=[pltpu.VMEM((v, n), BF16)] * (2 * n_split)
        + [pltpu.VMEM(s, F32) for s in extra],
        cost_estimate=pl.CostEstimate(
            flops=flops, bytes_accessed=1 << 20, transcendentals=0
        ),
        compiler_params=pltpu.CompilerParams(vmem_limit_bytes=24 << 20),
    )(*args)


def body(slabs, eps_occ, eps_vir):
    own = slabs[0]
    v = own.shape[0]
    n_orb, n_grp = lax.axis_size("orb"), lax.axis_size("grp")
    chunks = [own[a:b] for a, b in zip(CUTS[:-1], CUTS[1:])]
    lows = [shift(chunks[i], 1) for i in range(4)]
    highs = [shift(chunks[i], -1) for i in range(4)]
    e_low = shift(eps_occ, 1)
    e_high = shift(eps_occ, -1)
    e_far = shift(eps_occ, 2)
    fars = [shift(lows[0], 1), shift(lows[1], 1)]
    fars += [shift(highs[2], -1), shift(highs[3], -1)]

    def recip(energy):
        return 1.0 / (energy - eps_vir[:, None] - eps_vir[None, :])

    r_low = recip(eps_occ[0] + e_low[0])
    r_high = recip(eps_occ[0] + e_high[0])
    r_mid = recip(e_low[0] + e_high[0])
    r_far = recip(eps_occ[0] + e_far[0])

    core = lax.rem(lax.axis_index("grp"), 2).astype(jnp.int32)[None]
    half = v // n_orb // 2
    piece = (n_orb, half, v)
    keep, send, s_low, s_high = call(
        density_kernel,
        (piece, piece, (v, v), (v, v)),
        3,
        ((v, v),),
        1 << 32,
        (core, own, *lows, *highs, r_low, r_high, r_mid),
        scalars=1,
    )
    other = lax.ppermute(send, "grp", [(i, i ^ 1) for i in range(n_grp)])
    pieces = lax.all_to_all(
        keep + other, "orb", split_axis=0, concat_axis=0, tiled=True
    )
    share = jnp.sum(pieces, axis=0) * (1.0 / (n_orb * n_grp))
    copies = lax.all_to_all(
        jnp.broadcast_to(share[None], (n_grp,) + share.shape),
        "grp",
        split_axis=0,
        concat_axis=0,
        tiled=True,
    )
    density = jnp.sum(copies.reshape(n_grp // 2, 2 * half, v), axis=0)

    (near,) = call(
        near_kernel, (own.shape,), 2, (), 1 << 31, (*lows, *highs, s_low, s_high)
    )
    (grad,) = call(far_kernel, (own.shape,), 2, (), 1 << 31, (own, *fars, r_far, near))
    return grad[None], density


def solution(mesh):
    placed = (P(("grp", "orb"), None, None), P(("grp", "orb")), P())
    return jax.shard_map(
        body,
        mesh=mesh,
        in_specs=placed,
        out_specs=(P(("grp", "orb"), None, None), P("orb", None)),
        check_vma=False,
    )
```

```python
import jax
import jax.numpy as jnp
from jax import lax
from jax.experimental import pallas as pl
from jax.experimental.pallas import tpu as pltpu
from jax.sharding import PartitionSpec as P


RING = 4
CUTS = (0, 128, 256)
FAR = (0, 32, 128)
VMEM = pl.BlockSpec(memory_space=pltpu.VMEM)
SMEM = pl.BlockSpec(memory_space=pltpu.SMEM)
F32, BF16 = jnp.float32, jnp.bfloat16


def shift(value, step):
    size = lax.axis_size("orb")
    pairs = [
        (at, at // RING * RING + (at % RING + step) % RING) for at in range(size)
    ]
    return lax.ppermute(value, "orb", pairs)


def split(x):
    high = x.astype(BF16)
    return high, (x - high.astype(F32)).astype(BF16)


def mm(a, b, contract):
    dims = ((contract, ((), ())))
    dot = lambda p, q: lax.dot_general(p, q, dims, preferred_element_type=F32)
    return dot(a[0], b[0]) + (dot(a[0], b[1]) + dot(a[1], b[0]))


ROWS = ((1,), (1,))
PLAIN = ((1,), (0,))


def fill(chunks, high, low):
    at = 0
    for chunk in chunks:
        end = at + chunk.shape[0]
        high[at:end, :], low[at:end, :] = split(chunk[...])
        at = end


def density_kernel(core, own, *refs):
    lows, highs, (r_low, r_high, r_mid) = refs[:2], refs[2:4], refs[4:7]
    keep, send, oh, ol, lh, ll, hh, hl, dens = refs[7:]
    fill((own,), oh, ol)
    fill(lows, lh, ll)
    fill(highs, hh, hl)
    o, l, h = (oh[...], ol[...]), (lh[...], ll[...]), (hh[...], hl[...])

    def term(left, right, recip):
        t = mm(left, right, ROWS) * recip[...]
        return mm(split(t), split(2.0 * t - t.T), ROWS)

    dens[...] = term(o, l, r_low) + term(o, h, r_high) + term(l, h, r_mid)
    mine = core[0] * 8
    for at in range(16):
        keep[at] = dens[pl.ds(pl.multiple_of(at * 16 + mine, 8), 8), :]
        send[at] = dens[pl.ds(pl.multiple_of(at * 16 + 8 - mine, 8), 8), :]


def gradient(own, other, recip):
    t = mm(own, other, ROWS) * recip[...]
    return mm(split(2.0 * t - t.T), other, PLAIN)


def near_kernel(own, *refs):
    lows, highs, (r_low, r_high, grad, oh, ol, lh, ll, hh, hl) = (
        refs[:2],
        refs[2:4],
        refs[4:],
    )
    fill((own,), oh, ol)
    fill(lows, lh, ll)
    fill(highs, hh, hl)
    o, l, h = (oh[...], ol[...]), (lh[...], ll[...]), (hh[...], hl[...])
    grad[...] = gradient(o, l, r_low) + gradient(o, h, r_high)


def far_kernel(own, *refs):
    fars, (recip, near, grad, oh, ol, fh, fl) = refs[:4], refs[4:]
    fill((own,), oh, ol)
    fill(fars, fh, fl)
    grad[...] = near[...] + gradient((oh[...], ol[...]), (fh[...], fl[...]), recip)


def call(kernel, out, n_split, extra, flops, args, scalars=0):
    v, n = 256, 1024
    shapes = tuple(jax.ShapeDtypeStruct(s, F32) for s in out)
    return pl.pallas_call(
        kernel,
        out_shape=shapes,
        in_specs=[SMEM] * scalars + [VMEM] * (len(args) - scalars),
        out_specs=tuple(VMEM for _ in out),
        scratch_shapes=[pltpu.VMEM((v, n), BF16)] * (2 * n_split)
        + [pltpu.VMEM(s, F32) for s in extra],
        cost_estimate=pl.CostEstimate(
            flops=flops, bytes_accessed=1 << 20, transcendentals=0
        ),
        compiler_params=pltpu.CompilerParams(vmem_limit_bytes=20 << 20),
    )(*args)


def body(slabs, eps_occ, eps_vir):
    own = slabs[0]
    v = own.shape[0]
    n_orb, n_grp = lax.axis_size("orb"), lax.axis_size("grp")
    chunks = [own[a:b] for a, b in zip(CUTS[:-1], CUTS[1:])]
    lows = [shift(chunks[i], 1) for i in range(2)]
    highs = [shift(chunks[i], -1) for i in range(2)]
    e_low = shift(eps_occ, 1)
    e_high = shift(eps_occ, -1)
    e_far = shift(eps_occ, 2)
    cut = FAR[1]
    fars = [shift(lows[0][:cut], 1), shift(lows[0][cut:], 1)]
    fars += [shift(highs[1][:-cut], -1), shift(highs[1][-cut:], -1)]

    def recip(energy):
        return 1.0 / (energy - eps_vir[:, None] - eps_vir[None, :])

    r_low = recip(eps_occ[0] + e_low[0])
    r_high = recip(eps_occ[0] + e_high[0])
    r_mid = recip(e_low[0] + e_high[0])
    r_far = recip(eps_occ[0] + e_far[0])

    core = lax.rem(lax.axis_index("grp"), 2).astype(jnp.int32)[None]
    half = v // n_orb // 2
    piece = (n_orb, half, v)
    keep, send = call(
        density_kernel,
        (piece, piece),
        3,
        ((v, v),),
        1 << 32,
        (core, own, *lows, *highs, r_low, r_high, r_mid),
        scalars=1,
    )
    other = lax.ppermute(send, "grp", [(i, i ^ 1) for i in range(n_grp)])
    pieces = lax.all_to_all(
        keep + other, "orb", split_axis=0, concat_axis=0, tiled=True
    )
    share = jnp.sum(pieces, axis=0) * (1.0 / (n_orb * n_grp))
    copies = lax.all_to_all(
        jnp.broadcast_to(share[None], (n_grp,) + share.shape),
        "grp",
        split_axis=0,
        concat_axis=0,
        tiled=True,
    )
    density = jnp.sum(copies.reshape(n_grp // 2, 2 * half, v), axis=0)

    (near,) = call(
        near_kernel, (own.shape,), 3, (), 1 << 31, (own, *lows, *highs, r_low, r_high)
    )
    (grad,) = call(far_kernel, (own.shape,), 2, (), 1 << 31, (own, *fars, r_far, near))
    return grad[None], density


def solution(mesh):
    placed = (P(("grp", "orb"), None, None), P(("grp", "orb")), P())
    return jax.shard_map(
        body,
        mesh=mesh,
        in_specs=placed,
        out_specs=(P(("grp", "orb"), None, None), P("orb", None)),
        check_vma=False,
    )
```

```python
import jax
import jax.numpy as jnp
from jax import lax
from jax.experimental import pallas as pl
from jax.experimental.pallas import tpu as pltpu
from jax.sharding import PartitionSpec as P


RING = 4
EARLY = 96
VMEM = pl.BlockSpec(memory_space=pltpu.VMEM)
SMEM = pl.BlockSpec(memory_space=pltpu.SMEM)
HBM = pl.BlockSpec(memory_space=pltpu.MemorySpace.HBM)
F32, BF16 = jnp.float32, jnp.bfloat16
ROWS = ((1,), (1,))
PLAIN = ((1,), (0,))
MIB = 1 << 20


def shift(value, step):
    size = lax.axis_size("orb")
    pairs = [
        (at, at // RING * RING + (at % RING + step) % RING) for at in range(size)
    ]
    return lax.ppermute(value, "orb", pairs)


def split(x):
    high = x.astype(BF16)
    return high, (x - high.astype(F32)).astype(BF16)


def mm(a, b, contract):
    def dot(p, q):
        return lax.dot_general(p, q, (contract, ((), ())), preferred_element_type=F32)

    return dot(a[0], b[0]) + (dot(a[0], b[1]) + dot(a[1], b[0]))


def fill(chunks, high, low):
    at = 0
    for chunk in chunks:
        end = at + chunk.shape[0]
        high[at:end, :], low[at:end, :] = split(chunk[...])
        at = end
    return high[...], low[...]


def pair_base(eps_vir):
    row = jnp.broadcast_to(eps_vir[...], (eps_vir.shape[1],) * 2)
    return row + row.T


def amplitudes(left, right, energy, base):
    t = mm(left, right, ROWS) / (energy - base)
    return split(t), split(2.0 * t - t.T)


def density_kernel(core, own, *refs):
    lows, highs, (energy, eps_vir, keep, send) = refs[:2], refs[2:4], refs[4:8]
    oh, ol, lh, ll, hh, hl, dens = refs[8:]
    base = pair_base(eps_vir)
    o, l, h = fill((own,), oh, ol), fill(lows, lh, ll), fill(highs, hh, hl)
    total = None
    for at, (left, right) in enumerate(((o, l), (o, h), (l, h))):
        t, s = amplitudes(left, right, energy[at : at + 1, 0:1], base)
        part = mm(t, s, ROWS)
        total = part if total is None else total + part
    dens[...] = total
    mine = core[0] * 8
    for at in range(16):
        keep[at] = dens[pl.ds(pl.multiple_of(at * 16 + mine, 8), 8), :]
        send[at] = dens[pl.ds(pl.multiple_of(at * 16 + 8 - mine, 8), 8), :]


def near_kernel(own, *refs):
    lows, highs, (energy, eps_vir, grad) = refs[:2], refs[2:4], refs[4:7]
    oh, ol, lh, ll, hh, hl, total, sem = refs[7:]
    base = pair_base(eps_vir)
    o, l, h = fill((own,), oh, ol), fill(lows, lh, ll), fill(highs, hh, hl)
    _, s_low = amplitudes(o, l, energy[0:1, 0:1], base)
    _, s_high = amplitudes(o, h, energy[1:2, 0:1], base)
    total[...] = mm(s_low, l, PLAIN) + mm(s_high, h, PLAIN)
    out = pltpu.make_async_copy(total, grad, sem)
    out.start()
    out.wait()


def far_kernel(own, *refs):
    fars, (energy, eps_vir, near, grad) = refs[:4], refs[4:8]
    oh, ol, fh, fl, before, total, sem_in, sem_out = refs[8:]
    fetch = pltpu.make_async_copy(near, before, sem_in)
    fetch.start()
    base = pair_base(eps_vir)
    f = fill(fars, fh, fl)
    _, s = amplitudes(fill((own,), oh, ol), f, energy[3:4, 0:1], base)
    fetch.wait()
    blocks, width = 4, total.shape[1] // 4
    outs = []
    for at in range(blocks):
        cols = slice(at * width, (at + 1) * width)
        total[:, cols] = before[:, cols] + mm(s, (f[0][:, cols], f[1][:, cols]), PLAIN)
        outs.append(
            pltpu.make_async_copy(
                total.at[:, cols], grad.at[:, cols], sem_out.at[at]
            )
        )
        outs[-1].start()
    for out in outs:
        out.wait()


def fold_kernel(pieces, copies):
    total = pieces[0]
    for at in range(1, pieces.shape[0]):
        total = total + pieces[at]
    total = total * (1.0 / 256.0)
    for at in range(copies.shape[0]):
        copies[at] = total


def call(kernel, out, scratch, limit, flops, args, in_specs, out_specs):
    return pl.pallas_call(
        kernel,
        out_shape=tuple(
            pltpu.HBM(s, F32) if spec is HBM else jax.ShapeDtypeStruct(s, F32)
            for s, spec in zip(out, out_specs)
        ),
        in_specs=in_specs,
        out_specs=out_specs,
        scratch_shapes=scratch,
        cost_estimate=pl.CostEstimate(
            flops=flops, bytes_accessed=MIB, transcendentals=0
        ),
        compiler_params=pltpu.CompilerParams(vmem_limit_bytes=limit * MIB),
    )(*args)


def body(slabs, eps_occ, eps_vir):
    own = slabs[0]
    v, n = own.shape
    n_orb, n_grp = lax.axis_size("orb"), lax.axis_size("grp")
    mid = v // 2
    own_a = own[:mid]
    own_b = lax.optimization_barrier(slabs)[0, mid:]
    low_a = shift(own_a, 1)
    high_b = shift(own_b, -1)
    e_low = shift(eps_occ, 1)
    e_high = shift(eps_occ, -1)
    e_far = shift(eps_occ, 2)
    lows = (low_a, shift(own_b, 1))
    highs = (shift(own_a, -1), high_b)
    pieces = [low_a[:EARLY], high_b[-EARLY:]]
    pieces += [low_a[EARLY:], high_b[:-EARLY]]
    fars = (
        shift(pieces[0], 1),
        shift(pieces[2], 1),
        shift(pieces[3], -1),
        shift(pieces[1], -1),
    )
    row = lax.broadcasted_iota(jnp.int32, (8, 128), 0)
    first = jnp.where(row == 2, e_low, eps_occ)
    second = jnp.where(row == 0, e_low, jnp.where(row == 3, e_far, e_high))
    energy = first + second
    eps_row = eps_vir[None]

    core = lax.rem(lax.axis_index("grp"), 2).astype(jnp.int32)[None]
    half = v // n_orb // 2
    piece = (n_orb, half, v)
    wide = [pltpu.VMEM((v, n), BF16)]
    keep, send = call(
        density_kernel,
        (piece, piece),
        wide * 6 + [pltpu.VMEM((v, v), F32)],
        16,
        1 << 32,
        (core, own, *lows, *highs, energy, eps_row),
        [SMEM] + [VMEM] * 7,
        (VMEM, VMEM),
    )
    other = lax.ppermute(send, "grp", [(i, i ^ 1) for i in range(n_grp)])
    parts = lax.all_to_all(keep + other, "orb", split_axis=0, concat_axis=0, tiled=True)
    (copies,) = call(fold_kernel, (piece,), [], 4, 1 << 20, (parts,), [VMEM], (VMEM,))
    copies = lax.all_to_all(
        copies, "grp", split_axis=0, concat_axis=0, tiled=True
    )
    density = jnp.sum(copies.reshape(n_grp // 2, 2 * half, v), axis=0)

    (near,) = call(
        near_kernel,
        (own.shape,),
        wide * 6 + [pltpu.VMEM((v, n), F32), pltpu.SemaphoreType.DMA],
        16,
        1 << 31,
        (own, *lows, *highs, energy, eps_row),
        [VMEM] * 7,
        (HBM,),
    )
    (grad,) = call(
        far_kernel,
        (own.shape,),
        wide * 4
        + [pltpu.VMEM((v, n), F32)] * 2
        + [pltpu.SemaphoreType.DMA, pltpu.SemaphoreType.DMA((4,))],
        16,
        1 << 31,
        (own, *fars, energy, eps_row, pltpu.with_memory_space_constraint(near, pltpu.HBM)),
        [VMEM] * 7 + [HBM],
        (HBM,),
    )
    return grad[None], density


def solution(mesh):
    placed = (P(("grp", "orb"), None, None), P(("grp", "orb")), P())
    return jax.shard_map(
        body,
        mesh=mesh,
        in_specs=placed,
        out_specs=(P(("grp", "orb"), None, None), P("orb", None)),
        check_vma=False,
    )
```

```python
import jax
import jax.numpy as jnp
from jax import lax
from jax.experimental import pallas as pl
from jax.experimental.pallas import tpu as pltpu
from jax.sharding import PartitionSpec as P


RING = 4
VMEM = pl.BlockSpec(memory_space=pltpu.VMEM)
SMEM = pl.BlockSpec(memory_space=pltpu.SMEM)
HBM = pl.BlockSpec(memory_space=pltpu.HBM)
F32, BF16 = jnp.float32, jnp.bfloat16
ROWS = ((1,), (1,))
PLAIN = ((1,), (0,))
MIB = 1 << 20


def shift(value, step):
    size = lax.axis_size("orb")
    pairs = [
        (at, at // RING * RING + (at % RING + step) % RING) for at in range(size)
    ]
    return lax.ppermute(value, "orb", pairs)


def split(x):
    high = x.astype(BF16)
    return high, (x - high.astype(F32)).astype(BF16)


def mm(a, b, contract):
    def dot(p, q):
        return lax.dot_general(p, q, (contract, ((), ())), preferred_element_type=F32)

    return dot(a[0], b[0]) + (dot(a[0], b[1]) + dot(a[1], b[0]))


def fill(chunks, high, low):
    at = 0
    for chunk in chunks:
        end = at + chunk.shape[0]
        high[at:end, :], low[at:end, :] = split(chunk[...])
        at = end
    return high[...], low[...]


def pair_base(eps_vir):
    row = jnp.broadcast_to(eps_vir[...], (eps_vir.shape[1],) * 2)
    return row + row.T


def amplitudes(left, right, energy, base):
    t = mm(left, right, ROWS) / (energy - base)
    return split(t), split(2.0 * t - t.T)


def density_kernel(core, e_own, e_low, e_high, *refs):
    own, low, high, eps_vir, keep, send, oh, ol, lh, ll, hh, hl, dens = refs
    base = pair_base(eps_vir)
    o, l, h = fill((own,), oh, ol), fill((low,), lh, ll), fill((high,), hh, hl)
    total = None
    for left, right, energy in (
        (o, l, e_own[0] + e_low[0]),
        (o, h, e_own[0] + e_high[0]),
        (l, h, e_low[0] + e_high[0]),
    ):
        t, s = amplitudes(left, right, energy, base)
        part = mm(t, s, ROWS)
        total = part if total is None else total + part
    dens[...] = total
    mine = core[0] * 8
    for at in range(16):
        keep[at] = dens[pl.ds(pl.multiple_of(at * 16 + mine, 8), 8), :]
        send[at] = dens[pl.ds(pl.multiple_of(at * 16 + 8 - mine, 8), 8), :]


def near_kernel(e_own, e_low, e_high, own, low, high, eps_vir, grad, *scratch):
    oh, ol, lh, ll, hh, hl, total, sem = scratch
    base = pair_base(eps_vir)
    o, l, h = fill((own,), oh, ol), fill((low,), lh, ll), fill((high,), hh, hl)
    _, s_low = amplitudes(o, l, e_own[0] + e_low[0], base)
    _, s_high = amplitudes(o, h, e_own[0] + e_high[0], base)
    total[...] = mm(s_low, l, PLAIN) + mm(s_high, h, PLAIN)
    out = pltpu.make_async_copy(total, grad, sem)
    out.start()
    out.wait()


def far_kernel(e_own, e_far, eps_vir, own, far_a, far_b, near, grad, *scratch):
    mine, far, before, total, sem_in, sem_out = scratch
    half = far_a.shape[0]
    fetches = [
        pltpu.make_async_copy(own, mine, sem_in.at[0]),
        pltpu.make_async_copy(far_a, far.at[:half, :], sem_in.at[1]),
        pltpu.make_async_copy(far_b, far.at[half:, :], sem_in.at[2]),
        pltpu.make_async_copy(near, before, sem_in.at[3]),
    ]
    for fetch in fetches:
        fetch.start()
    base = pair_base(eps_vir)
    fetches[0].wait()
    o = split(mine[...])
    fetches[1].wait()
    fetches[2].wait()
    f = split(far[...])
    _, s = amplitudes(o, f, e_own[0] + e_far[0], base)
    fetches[3].wait()
    blocks = 4
    width = total.shape[1] // blocks
    outs = []
    for at in range(blocks):
        cols = slice(at * width, (at + 1) * width)
        total[:, cols] = before[:, cols] + mm(s, (f[0][:, cols], f[1][:, cols]), PLAIN)
        outs.append(
            pltpu.make_async_copy(
                total.at[:, cols], grad.at[:, cols], sem_out.at[at]
            )
        )
        outs[-1].start()
    for out in outs:
        out.wait()


def fold_kernel(pieces, copies):
    total = pieces[0]
    for at in range(1, pieces.shape[0]):
        total = total + pieces[at]
    total = total * (1.0 / 256.0)
    for at in range(copies.shape[0]):
        copies[at] = total


def call(kernel, out, scratch, limit, flops, args, in_specs, out_specs):
    return pl.pallas_call(
        kernel,
        out_shape=tuple(
            pltpu.HBM(s, F32) if spec is HBM else jax.ShapeDtypeStruct(s, F32)
            for s, spec in zip(out, out_specs)
        ),
        in_specs=in_specs,
        out_specs=out_specs,
        scratch_shapes=scratch,
        cost_estimate=pl.CostEstimate(
            flops=flops, bytes_accessed=MIB, transcendentals=0
        ),
        compiler_params=pltpu.CompilerParams(vmem_limit_bytes=limit * MIB),
    )(*args)


def body(slabs, eps_occ, eps_vir):
    own = slabs[0]
    v, n = own.shape
    n_orb, n_grp = lax.axis_size("orb"), lax.axis_size("grp")
    mid = v // 2
    low = shift(own, 1)
    high = shift(own, -1)
    e_low = shift(eps_occ, 1)
    e_high = shift(eps_occ, -1)
    e_far = shift(e_low, 1)
    low_a, high_b = low[:mid], high[mid:]
    far_a = shift(low_a, 1)
    far_b = shift(high_b, -1)
    eps_row = eps_vir[None]

    core = lax.rem(lax.axis_index("grp"), 2).astype(jnp.int32)[None]
    half = v // n_orb // 2
    piece = (n_orb, half, v)
    wide = [pltpu.VMEM((v, n), BF16)]
    full = [pltpu.VMEM((v, n), F32)]
    keep, send = call(
        density_kernel,
        (piece, piece),
        wide * 6 + [pltpu.VMEM((v, v), F32)],
        16,
        1 << 32,
        (core, eps_occ, e_low, e_high, own, low, high, eps_row),
        [SMEM] * 4 + [VMEM] * 4,
        (VMEM, VMEM),
    )
    other = lax.ppermute(send, "grp", [(i, i ^ 1) for i in range(n_grp)])
    parts = lax.all_to_all(keep + other, "orb", split_axis=0, concat_axis=0, tiled=True)
    (copies,) = call(fold_kernel, (piece,), [], 4, 1 << 20, (parts,), [VMEM], (VMEM,))
    copies = lax.all_to_all(
        copies, "grp", split_axis=0, concat_axis=0, tiled=True
    )
    density = jnp.sum(copies.reshape(n_grp // 2, 2 * half, v), axis=0)

    (near,) = call(
        near_kernel,
        (own.shape,),
        wide * 6 + full + [pltpu.SemaphoreType.DMA],
        16,
        1 << 31,
        (eps_occ, e_low, e_high, own, low, high, eps_row),
        [SMEM] * 3 + [VMEM] * 4,
        (HBM,),
    )
    hold = [pltpu.with_memory_space_constraint(x, pltpu.HBM) for x in (near,)]
    (grad,) = call(
        far_kernel,
        (own.shape,),
        full * 4 + [pltpu.SemaphoreType.DMA((4,))] * 2,
        16,
        1 << 31,
        (eps_occ, e_far, eps_row, own, far_a, far_b, *hold),
        [SMEM] * 2 + [VMEM] + [HBM] * 4,
        (HBM,),
    )
    return grad[None], density


def solution(mesh):
    placed = (P(("grp", "orb"), None, None), P(("grp", "orb")), P())
    return jax.shard_map(
        body,
        mesh=mesh,
        in_specs=placed,
        out_specs=(P(("grp", "orb"), None, None), P("orb", None)),
        check_vma=False,
    )
```

```python
import jax
import jax.numpy as jnp
from jax import lax
from jax.experimental import pallas as pl
from jax.experimental.pallas import tpu as pltpu
from jax.sharding import Mesh, PartitionSpec as P


FINE = ("y", "near", "core", "x", "far")
FINE_SHAPE = (4, 2, 2, 4, 4)
VMEM = pl.BlockSpec(memory_space=pltpu.VMEM)
SMEM = pl.BlockSpec(memory_space=pltpu.SMEM)
HBM = pl.BlockSpec(memory_space=pltpu.HBM)
F32, BF16 = jnp.float32, jnp.bfloat16
ROWS = ((1,), (1,))
PLAIN = ((1,), (0,))
MIB = 1 << 20


def shift(value, step):
    size = lax.axis_size("far")
    return lax.ppermute(value, "far", [(i, (i + step) % size) for i in range(size)])


def split(x):
    high = x.astype(BF16)
    return high, (x - high.astype(F32)).astype(BF16)


def mm(a, b, contract):
    def dot(p, q):
        return lax.dot_general(p, q, (contract, ((), ())), preferred_element_type=F32)

    return dot(a[0], b[0]) + (dot(a[0], b[1]) + dot(a[1], b[0]))


def fill(chunks, high, low):
    at = 0
    for chunk in chunks:
        end = at + chunk.shape[0]
        high[at:end, :], low[at:end, :] = split(chunk[...])
        at = end
    return high[...], low[...]


def base_kernel(eps_vir, base):
    row = jnp.broadcast_to(eps_vir[...], base.shape)
    base[...] = row + row.T


def join_kernel(keep, other, copies):
    for at in range(copies.shape[1]):
        piece = keep[at] + other[at]
        for copy in range(copies.shape[0]):
            copies[copy, at] = piece


def amplitudes(left, right, energy, base):
    return mm(left, right, ROWS) / (energy - base)


def spin(t):
    return split(2.0 * t - t.T)


def density_kernel(
    core, e_own, e_low, e_high, pairs, own, low, high, keep, send, down, up, *scratch
):
    oh, ol, lh, ll, hh, hl, dens, buf_down, buf_up, mine, sems = scratch
    half = down.shape[0]
    fetch = pltpu.make_async_copy(own, mine, sems.at[2])
    fetch.start()
    base = pairs[...]
    l, h = fill((low,), lh, ll), fill((high,), hh, hl)
    t = amplitudes(l, h, e_low[...] + e_high[...], base)
    s, r = spin(t), split(2.0 * t.T - t)
    buf_down[...] = mm([x[:half] for x in s], h, PLAIN)
    to_down = pltpu.make_async_copy(buf_down, down, sems.at[0])
    to_down.start()
    buf_up[...] = mm([x[half:] for x in r], l, PLAIN)
    to_up = pltpu.make_async_copy(buf_up, up, sems.at[1])
    to_up.start()
    total = mm(split(t), s, ROWS)
    fetch.wait()
    o = fill((mine,), oh, ol)
    for other, energy in ((l, e_low), (h, e_high)):
        t = amplitudes(o, other, e_own[...] + energy[...], base)
        total = total + mm(split(t), spin(t), ROWS)
    dens[...] = total
    first = core[0] * 8
    for at in range(16):
        keep[at] = dens[pl.ds(pl.multiple_of(at * 16 + first, 8), 8), :]
        send[at] = dens[pl.ds(pl.multiple_of(at * 16 + 8 - first, 8), 8), :]
    to_down.wait()
    to_up.wait()


def near_kernel(e_own, e_low, e_high, pairs, own, low, high, grad, *scratch):
    oh, ol, lh, ll, hh, hl, total, sem = scratch
    base = pairs[...]
    fetch = pltpu.make_async_copy(own, total, sem)
    fetch.start()
    l, h = fill((low,), lh, ll), fill((high,), hh, hl)
    fetch.wait()
    o = fill((total,), oh, ol)
    s_low = spin(amplitudes(o, l, e_own[...] + e_low[...], base))
    s_high = spin(amplitudes(o, h, e_own[...] + e_high[...], base))
    total[...] = mm(s_low, l, PLAIN) + mm(s_high, h, PLAIN)
    out = pltpu.make_async_copy(total, grad, sem)
    out.start()
    out.wait()


def sum_kernel(near, first, second, grad, mine, other, sems):
    half = first.shape[0]
    parts, step = 4, half // 2
    copies = []
    for at in range(parts):
        rows = pl.ds(at * step, step)
        source = (first, second)[at // 2].at[pl.ds(at % 2 * step, step), :]
        copies.append(
            (
                pltpu.make_async_copy(near.at[rows, :], mine.at[rows, :], sems.at[0, at]),
                pltpu.make_async_copy(source, other.at[rows, :], sems.at[1, at]),
                pltpu.make_async_copy(mine.at[rows, :], grad.at[rows, :], sems.at[2, at]),
            )
        )
        copies[-1][0].start()
        copies[-1][1].start()
    for at in range(parts):
        rows = slice(at * step, (at + 1) * step)
        copies[at][0].wait()
        copies[at][1].wait()
        mine[rows, :] = mine[rows, :] + other[rows, :]
        copies[at][2].start()
    for at in range(parts):
        copies[at][2].wait()


def fold_kernel(pieces, copies):
    total = pieces[0]
    for at in range(1, pieces.shape[0]):
        total = total + pieces[at]
    total = total * (1.0 / 256.0)
    for at in range(copies.shape[0]):
        row = at // 2 % 4 * 8
        copies[at] = total[row : row + 8, :]


def call(kernel, out, scratch, limit, flops, args, in_specs, out_specs):
    return pl.pallas_call(
        kernel,
        out_shape=tuple(
            pltpu.HBM(s, F32) if spec is HBM else jax.ShapeDtypeStruct(s, F32)
            for s, spec in zip(out, out_specs)
        ),
        in_specs=in_specs,
        out_specs=out_specs,
        scratch_shapes=scratch,
        cost_estimate=pl.CostEstimate(
            flops=flops, bytes_accessed=MIB, transcendentals=0
        ),
        compiler_params=pltpu.CompilerParams(vmem_limit_bytes=limit * MIB),
    )(*args)


def body(slabs, eps_occ, eps_vir):
    own = slabs[0]
    v, n = own.shape
    low = shift(own, 1)
    high = shift(own, -1)
    e_own = eps_occ[None]
    e_low = shift(eps_occ, 1)[None]
    e_high = shift(eps_occ, -1)[None]
    (pairs,) = call(base_kernel, ((v, v),), [], 4, 1 << 20, (eps_vir[None],), [VMEM], (VMEM,))

    source = pltpu.with_memory_space_constraint(own, pltpu.HBM)
    core = lax.axis_index("core").astype(jnp.int32)[None]
    piece = (16, 8, v)
    wide = [pltpu.VMEM((v, n), BF16)]
    full = [pltpu.VMEM((v, n), F32)]
    part = [pltpu.VMEM((v // 2, n), F32)]
    keep, send, down, up = call(
        density_kernel,
        (piece, piece, (v // 2, n), (v // 2, n)),
        wide * 6 + [pltpu.VMEM((v, v), F32)] + part * 2 + full + [pltpu.SemaphoreType.DMA((3,))],
        16,
        1 << 32,
        (core, e_own, e_low, e_high, pairs, source, low, high),
        [SMEM] + [VMEM] * 4 + [HBM] + [VMEM] * 2,
        (VMEM, VMEM, HBM, HBM),
    )
    other = lax.ppermute(send, "core", [(0, 1), (1, 0)])
    second = shift(up, 1)
    first = shift(down, -1)
    (mine,) = call(join_kernel, ((4,) + piece,), [], 4, 1 << 20, (keep, other), [VMEM] * 2, (VMEM,))
    parts = lax.all_to_all(
        mine.reshape(16, 32, v),
        ("y", "x"),
        split_axis=0,
        concat_axis=0,
        tiled=True,
    )
    (copies,) = call(fold_kernel, (piece,), [], 4, 1 << 20, (parts,), [VMEM], (VMEM,))
    copies = lax.all_to_all(
        copies, ("near", "far", "core"), split_axis=0, concat_axis=0, tiled=True
    )
    density = jnp.sum(copies.reshape(8, 16, v), axis=0)

    (near,) = call(
        near_kernel,
        (own.shape,),
        wide * 6 + full + [pltpu.SemaphoreType.DMA],
        16,
        1 << 31,
        (e_own, e_low, e_high, pairs, source, low, high),
        [VMEM] * 4 + [HBM] + [VMEM] * 2,
        (HBM,),
    )
    near = pltpu.with_memory_space_constraint(near, pltpu.HBM)
    (grad,) = call(
        sum_kernel,
        (own.shape,),
        full * 2 + [pltpu.SemaphoreType.DMA((3, 4))],
        8,
        1 << 20,
        (near, first, second),
        [HBM] * 3,
        (HBM,),
    )
    return grad[None], density


def solution(mesh):
    fine = Mesh(mesh.devices.reshape(FINE_SHAPE), FINE)
    placed = (P(FINE, None, None), P(FINE), P())
    return jax.shard_map(
        body,
        mesh=fine,
        in_specs=placed,
        out_specs=(P(FINE, None, None), P(("x", "far"), None)),
        check_vma=False,
    )
```

```python
import jax
import jax.numpy as jnp
from jax import lax
from jax.experimental import pallas as pl
from jax.experimental.pallas import tpu as pltpu
from jax.sharding import Mesh, PartitionSpec as P


FINE = ("y", "near", "core", "x", "far")
FINE_SHAPE = (4, 2, 2, 4, 4)
VMEM = pl.BlockSpec(memory_space=pltpu.VMEM)
SMEM = pl.BlockSpec(memory_space=pltpu.SMEM)
HBM = pl.BlockSpec(memory_space=pltpu.HBM)
F32, BF16 = jnp.float32, jnp.bfloat16
ROWS = ((1,), (1,))
PLAIN = ((1,), (0,))
MIB = 1 << 20


def shift(value, step):
    size = lax.axis_size("far")
    return lax.ppermute(value, "far", [(i, (i + step) % size) for i in range(size)])


def split(x):
    high = x.astype(BF16)
    return high, (x - high.astype(F32)).astype(BF16)


def mm(a, b, contract):
    def dot(p, q):
        return lax.dot_general(p, q, (contract, ((), ())), preferred_element_type=F32)

    return dot(a[0], b[0]) + (dot(a[0], b[1]) + dot(a[1], b[0]))


def fill(chunks, high, low):
    at = 0
    for chunk in chunks:
        end = at + chunk.shape[0]
        high[at:end, :], low[at:end, :] = split(chunk[...])
        at = end
    return high[...], low[...]


def base_kernel(eps_vir, base):
    row = jnp.broadcast_to(eps_vir[...], base.shape)
    base[...] = row + row.T


def join_kernel(keep, other, copies):
    for at in range(copies.shape[1]):
        piece = keep[at] + other[at]
        for copy in range(copies.shape[0]):
            copies[copy, at] = piece


def spin(t):
    return split(2.0 * t - t.T)


def scalars(refs, values, sems):
    copies = [
        pltpu.make_async_copy(ref, value, sems.at[at])
        for at, (ref, value) in enumerate(zip(refs, values))
    ]
    for copy in copies:
        copy.start()
    return copies


def mid_kernel(e_low, e_high, pairs, low, high, down, up, *scratch):
    lh, ll, hh, hl, buf_down, buf_up, s_low, s_high, small, sems = scratch
    copies = scalars((e_low, e_high), (s_low, s_high), small)
    half = down.shape[0]
    l, h = fill((low,), lh, ll), fill((high,), hh, hl)
    k = mm(l, h, ROWS)
    for copy in copies:
        copy.wait()
    t = k / (s_low[0] + s_high[0] - pairs[...])
    turned = t.T
    s = split(2.0 * t[:half] - turned[:half])
    buf_down[...] = mm(s, h, PLAIN)
    to_down = pltpu.make_async_copy(buf_down, down, sems.at[0])
    to_down.start()
    s = split(2.0 * turned[half:] - t[half:])
    buf_up[...] = mm(s, l, PLAIN)
    to_up = pltpu.make_async_copy(buf_up, up, sems.at[1])
    to_up.start()
    to_down.wait()
    to_up.wait()


def density_kernel(
    e_own, core, e_low, e_high, pairs, own, low, high, keep, send, *scratch
):
    oh, ol, lh, ll, hh, hl, dens, mine, sem, c, s_low, s_high, small = scratch
    copies = scalars((core, e_low, e_high), (c, s_low, s_high), small)
    fetch = pltpu.make_async_copy(own, mine, sem)
    fetch.start()
    l, h = fill((low,), lh, ll), fill((high,), hh, hl)
    k = mm(l, h, ROWS)
    for copy in copies:
        copy.wait()
    t = k / (s_low[0] + s_high[0] - pairs[...])
    total = mm(split(t), spin(t), ROWS)
    fetch.wait()
    o = fill((mine,), oh, ol)
    for other, energy in ((l, s_low), (h, s_high)):
        t = mm(o, other, ROWS) / (e_own[0] + energy[0] - pairs[...])
        total = total + mm(split(t), spin(t), ROWS)
    dens[...] = total
    first = c[0] * 8
    for at in range(16):
        keep[at] = dens[pl.ds(pl.multiple_of(at * 16 + first, 8), 8), :]
        send[at] = dens[pl.ds(pl.multiple_of(at * 16 + 8 - first, 8), 8), :]


def near_kernel(e_own, e_low, e_high, pairs, own, low, high, grad, *scratch):
    oh, ol, lh, ll, hh, hl, total, sem, s_low, s_high, small = scratch
    copies = scalars((e_low, e_high), (s_low, s_high), small)
    fetch = pltpu.make_async_copy(own, total, sem)
    fetch.start()
    l, h = fill((low,), lh, ll), fill((high,), hh, hl)
    fetch.wait()
    o = fill((total,), oh, ol)
    for copy in copies:
        copy.wait()
    parts = [
        spin(mm(o, other, ROWS) / (e_own[0] + energy[0] - pairs[...]))
        for other, energy in ((l, s_low), (h, s_high))
    ]
    total[...] = mm(parts[0], l, PLAIN) + mm(parts[1], h, PLAIN)
    out = pltpu.make_async_copy(total, grad, sem)
    out.start()
    out.wait()


def sum_kernel(near, first, second, grad, mine, other, sems):
    half = first.shape[0]
    parts, step = 4, half // 2
    copies = []
    for at in range(parts):
        rows = pl.ds(at * step, step)
        source = (first, second)[at // 2].at[pl.ds(at % 2 * step, step), :]
        copies.append(
            (
                pltpu.make_async_copy(near.at[rows, :], mine.at[rows, :], sems.at[0, at]),
                pltpu.make_async_copy(source, other.at[rows, :], sems.at[1, at]),
                pltpu.make_async_copy(mine.at[rows, :], grad.at[rows, :], sems.at[2, at]),
            )
        )
        copies[-1][0].start()
        copies[-1][1].start()
    for at in range(parts):
        rows = slice(at * step, (at + 1) * step)
        copies[at][0].wait()
        copies[at][1].wait()
        mine[rows, :] = mine[rows, :] + other[rows, :]
        copies[at][2].start()
    for at in range(parts):
        copies[at][2].wait()


def fold_kernel(pieces, copies):
    total = pieces[0]
    for at in range(1, pieces.shape[0]):
        total = total + pieces[at]
    total = total * (1.0 / 256.0)
    for at in range(copies.shape[0]):
        row = at // 2 % 4 * 8
        copies[at] = total[row : row + 8, :]


def call(kernel, out, scratch, limit, flops, args, in_specs, out_specs):
    return pl.pallas_call(
        kernel,
        out_shape=tuple(
            pltpu.HBM(s, F32) if spec is HBM else jax.ShapeDtypeStruct(s, F32)
            for s, spec in zip(out, out_specs)
        ),
        in_specs=in_specs,
        out_specs=out_specs,
        scratch_shapes=scratch,
        cost_estimate=pl.CostEstimate(
            flops=flops, bytes_accessed=MIB, transcendentals=0
        ),
        compiler_params=pltpu.CompilerParams(vmem_limit_bytes=limit * MIB),
    )(*args)


def in_hbm(x):
    return pltpu.with_memory_space_constraint(x, pltpu.HBM)


def body(slabs, eps_occ, eps_vir):
    own = slabs[0]
    v, n = own.shape
    low = shift(own, 1)
    high = shift(own, -1)
    e_own = eps_occ
    e_low = shift(eps_occ, 1)
    e_high = shift(eps_occ, -1)
    (pairs,) = call(
        base_kernel, ((v, v),), [], 4, 1 << 20, (eps_vir[None],), [VMEM], (VMEM,)
    )

    source = in_hbm(own)
    core = lax.axis_index("core").astype(jnp.int32)[None]
    piece = (16, 8, v)
    wide = [pltpu.VMEM((v, n), BF16)]
    full = [pltpu.VMEM((v, n), F32)]
    part = [pltpu.VMEM((v // 2, n), F32)]
    one = pltpu.SMEM((1,), F32)
    down, up = call(
        mid_kernel,
        ((v // 2, n), (v // 2, n)),
        wide * 4 + part * 2 + [one] * 2 + [pltpu.SemaphoreType.DMA((2,))] * 2,
        12,
        1 << 31,
        (e_low, e_high, pairs, low, high),
        [HBM] * 2 + [VMEM] * 3,
        (HBM, HBM),
    )
    first = shift(down, -1)
    second = in_hbm(shift(up, 1))
    keep, send = call(
        density_kernel,
        (piece, piece),
        wide * 6
        + [pltpu.VMEM((v, v), F32)]
        + full
        + [pltpu.SemaphoreType.DMA, pltpu.SMEM((1,), jnp.int32)]
        + [one] * 2
        + [pltpu.SemaphoreType.DMA((3,))],
        16,
        1 << 31,
        (e_own, core, e_low, e_high, pairs, source, low, high),
        [SMEM] + [HBM] * 3 + [VMEM] + [HBM] + [VMEM] * 2,
        (VMEM, VMEM),
    )
    other = lax.ppermute(send, "core", [(0, 1), (1, 0)])
    (mine,) = call(
        join_kernel, ((4,) + piece,), [], 4, 1 << 20, (keep, other), [VMEM] * 2, (VMEM,)
    )
    parts = lax.all_to_all(
        mine.reshape(16, 32, v),
        ("y", "x"),
        split_axis=0,
        concat_axis=0,
        tiled=True,
    )
    (copies,) = call(fold_kernel, (piece,), [], 4, 1 << 20, (parts,), [VMEM], (VMEM,))
    copies = lax.all_to_all(
        copies, ("near", "far", "core"), split_axis=0, concat_axis=0, tiled=True
    )
    density = jnp.sum(copies.reshape(8, 16, v), axis=0)

    (near,) = call(
        near_kernel,
        (own.shape,),
        wide * 6
        + full
        + [pltpu.SemaphoreType.DMA]
        + [one] * 2
        + [pltpu.SemaphoreType.DMA((2,))],
        16,
        1 << 31,
        (e_own, e_low, e_high, pairs, source, low, high),
        [SMEM] + [HBM] * 2 + [VMEM] + [HBM] + [VMEM] * 2,
        (HBM,),
    )
    near = in_hbm(near)
    (grad,) = call(
        sum_kernel,
        (own.shape,),
        full * 2 + [pltpu.SemaphoreType.DMA((3, 4))],
        8,
        1 << 20,
        (near, first, second),
        [HBM] * 3,
        (HBM,),
    )
    return grad[None], density


def solution(mesh):
    fine = Mesh(mesh.devices.reshape(FINE_SHAPE), FINE)
    placed = (P(FINE, None, None), P(FINE), P())
    return jax.shard_map(
        body,
        mesh=fine,
        in_specs=placed,
        out_specs=(P(FINE, None, None), P(("x", "far"), None)),
        check_vma=False,
    )
```

```python
import jax
import jax.numpy as jnp
from jax import lax
from jax.experimental import pallas as pl
from jax.experimental.pallas import tpu as pltpu
from jax.sharding import Mesh, PartitionSpec as P


FINE = ("y", "near", "core", "x", "far")
FINE_SHAPE = (4, 2, 2, 4, 4)
VMEM = pl.BlockSpec(memory_space=pltpu.VMEM)
SMEM = pl.BlockSpec(memory_space=pltpu.SMEM)
HBM = pl.BlockSpec(memory_space=pltpu.HBM)
F32, BF16 = jnp.float32, jnp.bfloat16
ROWS = ((1,), (1,))
PLAIN = ((1,), (0,))
MIB = 1 << 20


def shift(value, step):
    size = lax.axis_size("far")
    return lax.ppermute(value, "far", [(i, (i + step) % size) for i in range(size)])


def split(x):
    high = x.astype(BF16)
    return high, (x - high.astype(F32)).astype(BF16)


def mm(a, b, contract):
    def dot(p, q):
        return lax.dot_general(p, q, (contract, ((), ())), preferred_element_type=F32)

    return dot(a[0], b[0]) + (dot(a[0], b[1]) + dot(a[1], b[0]))


def prepare_kernel(eps_vir, own, pairs, high, low):
    row = jnp.broadcast_to(eps_vir[...], pairs.shape)
    pairs[...] = row + row.T
    high[...], low[...] = split(own[...])


def spin(t):
    return split(2.0 * t - t.T)


def mid_kernel(energy, pairs, low, high, down, up, t_mid, lh, ll, hh, hl, *scratch):
    buf_down, buf_up, sems = scratch
    half = down.shape[0]
    lh[...], ll[...] = l = split(low[...])
    hh[...], hl[...] = h = split(high[...])
    t = mm(l, h, ROWS) / (energy[0:1, 0:1] - pairs[...])
    turned = t.T
    s = split(2.0 * t[:half] - turned[:half])
    buf_down[...] = mm(s, h, PLAIN)
    to_down = pltpu.make_async_copy(buf_down, down, sems.at[0])
    to_down.start()
    s = split(2.0 * turned[half:] - t[half:])
    buf_up[...] = mm(s, l, PLAIN)
    to_up = pltpu.make_async_copy(buf_up, up, sems.at[1])
    to_up.start()
    t_mid[...] = t
    to_down.wait()
    to_up.wait()


def density_kernel(
    upper, e_low, e_high, pairs, t_mid, oh, ol, lh, ll, hh, hl, keep, send, dens
):
    o, l, h = (oh[...], ol[...]), (lh[...], ll[...]), (hh[...], hl[...])
    t = t_mid[...]
    total = mm(split(t), spin(t), ROWS)
    for other, energy in ((l, e_low), (h, e_high)):
        t = mm(o, other, ROWS) / (energy[0:1, 0:1] - pairs[...])
        total = total + mm(split(t), spin(t), ROWS)
    dens[...] = total
    mine = upper[...] > 0.5
    for at in range(16):
        first = dens[at * 16 : at * 16 + 8, :]
        second = dens[at * 16 + 8 : at * 16 + 16, :]
        keep[at] = jnp.where(mine, second, first)
        send[at] = jnp.where(mine, first, second)


def near_kernel(e_low, e_high, pairs, oh, ol, lh, ll, hh, hl, grad, total, sem):
    o, l, h = (oh[...], ol[...]), (lh[...], ll[...]), (hh[...], hl[...])
    parts = [
        spin(mm(o, other, ROWS) / (energy[0:1, 0:1] - pairs[...]))
        for other, energy in ((l, e_low), (h, e_high))
    ]
    total[...] = mm(parts[0], l, PLAIN) + mm(parts[1], h, PLAIN)
    out = pltpu.make_async_copy(total, grad, sem)
    out.start()
    out.wait()


def sum_kernel(near, first, second, grad, mine, other, sems):
    half = first.shape[0]
    parts, step = 4, half // 2
    copies = []
    for at in range(parts):
        rows = pl.ds(at * step, step)
        source = (first, second)[at // 2].at[pl.ds(at % 2 * step, step), :]
        copies.append(
            (
                pltpu.make_async_copy(near.at[rows, :], mine.at[rows, :], sems.at[0, at]),
                pltpu.make_async_copy(source, other.at[rows, :], sems.at[1, at]),
                pltpu.make_async_copy(mine.at[rows, :], grad.at[rows, :], sems.at[2, at]),
            )
        )
        copies[-1][0].start()
        copies[-1][1].start()
    for at in range(parts):
        rows = slice(at * step, (at + 1) * step)
        copies[at][0].wait()
        copies[at][1].wait()
        mine[rows, :] = mine[rows, :] + other[rows, :]
        copies[at][2].start()
    for at in range(parts):
        copies[at][2].wait()


def fold_kernel(pieces, copies):
    total = pieces[0]
    for at in range(1, pieces.shape[0]):
        total = total + pieces[at]
    total = total * (1.0 / 256.0)
    for at in range(copies.shape[0]):
        copies[at] = total


def call(kernel, out, scratch, limit, flops, args, in_specs, out_specs):
    return pl.pallas_call(
        kernel,
        out_shape=tuple(
            pltpu.HBM(s, F32)
            if spec is HBM
            else jax.ShapeDtypeStruct(s, BF16 if s == (256, 1024) else F32)
            for s, spec in zip(out, out_specs)
        ),
        in_specs=in_specs,
        out_specs=out_specs,
        scratch_shapes=scratch,
        cost_estimate=pl.CostEstimate(
            flops=flops, bytes_accessed=MIB, transcendentals=0
        ),
        compiler_params=pltpu.CompilerParams(vmem_limit_bytes=limit * MIB),
    )(*args)


def in_hbm(x):
    return pltpu.with_memory_space_constraint(x, pltpu.HBM)


def body(slabs, eps_occ, eps_vir):
    own = slabs[0]
    v, n = own.shape
    low = shift(own, 1)
    high = shift(own, -1)
    tile = (8, 128)
    e_low, e_high = shift(eps_occ, 1), shift(eps_occ, -1)
    s_low = jnp.broadcast_to(eps_occ + e_low, tile)
    s_high = jnp.broadcast_to(eps_occ + e_high, tile)
    s_mid = jnp.broadcast_to(e_low + e_high, tile)
    upper = jnp.broadcast_to(lax.axis_index("core").astype(F32), (8, v))
    pairs, oh, ol = call(
        prepare_kernel,
        ((v, v), (v, n), (v, n)),
        [],
        8,
        1 << 20,
        (eps_vir[None], own),
        [VMEM] * 2,
        (VMEM,) * 3,
    )
    piece = (16, 8, v)
    part = [pltpu.VMEM((v // 2, n), F32)]
    down, up, t_mid, *splits = call(
        mid_kernel,
        ((v // 2, n), (v // 2, n), (v, v)) + ((v, n),) * 4,
        part * 2 + [pltpu.SemaphoreType.DMA((2,))],
        12,
        1 << 31,
        (s_mid, pairs, low, high),
        [VMEM] * 4,
        (HBM, HBM) + (VMEM,) * 5,
    )
    first = shift(down, -1)
    second = in_hbm(shift(up, 1))
    keep, send = call(
        density_kernel,
        (piece, piece),
        [pltpu.VMEM((v, v), F32)],
        12,
        1 << 31,
        (upper, s_low, s_high, pairs, t_mid, oh, ol, *splits),
        [VMEM] * 11,
        (VMEM, VMEM),
    )
    other = lax.ppermute(send, "core", [(0, 1), (1, 0)])
    parts = lax.all_to_all(
        keep + other, ("x", "far"), split_axis=0, concat_axis=0, tiled=True
    )
    (copies,) = call(fold_kernel, (piece,), [], 4, 1 << 20, (parts,), [VMEM], (VMEM,))
    copies = lax.all_to_all(
        copies, ("y", "near", "core"), split_axis=0, concat_axis=0, tiled=True
    )
    density = jnp.sum(copies.reshape(8, 16, v), axis=0)

    (near,) = call(
        near_kernel,
        ((v, n),),
        [pltpu.VMEM((v, n), F32), pltpu.SemaphoreType.DMA],
        12,
        1 << 31,
        (s_low, s_high, pairs, oh, ol, *splits),
        [VMEM] * 9,
        (HBM,),
    )
    (grad,) = call(
        sum_kernel,
        ((v, n),),
        [pltpu.VMEM((v, n), F32)] * 2 + [pltpu.SemaphoreType.DMA((3, 4))],
        8,
        1 << 20,
        (in_hbm(near), first, second),
        [HBM] * 3,
        (HBM,),
    )
    return grad[None], density


def solution(mesh):
    fine = Mesh(mesh.devices.reshape(FINE_SHAPE), FINE)
    placed = (P(FINE, None, None), P(FINE), P())
    return jax.shard_map(
        body,
        mesh=fine,
        in_specs=placed,
        out_specs=(P(FINE, None, None), P(("x", "far"), None)),
        check_vma=False,
    )
```

```python
import jax
import jax.numpy as jnp
from jax import lax
from jax.experimental import pallas as pl
from jax.experimental.pallas import tpu as pltpu
from jax.sharding import Mesh, PartitionSpec as P


FINE = ("y", "near", "core", "x", "far")
FINE_SHAPE = (4, 2, 2, 4, 4)
VMEM = pl.BlockSpec(memory_space=pltpu.VMEM)
SMEM = pl.BlockSpec(memory_space=pltpu.SMEM)
HBM = pl.BlockSpec(memory_space=pltpu.HBM)
F32, BF16 = jnp.float32, jnp.bfloat16
ROWS = ((1,), (1,))
PLAIN = ((1,), (0,))
MIB = 1 << 20


def shift(value, step):
    size = lax.axis_size("far")
    return lax.ppermute(value, "far", [(i, (i + step) % size) for i in range(size)])


def give(value, step, core):
    size = lax.axis_size("far")
    pairs = [(core * size + i, core * size + (i + step) % size) for i in range(size)]
    return lax.ppermute(value, ("core", "far"), pairs)


def split(x):
    high = x.astype(BF16)
    return high, (x - high.astype(F32)).astype(BF16)


def mm(a, b, contract):
    def dot(p, q):
        return lax.dot_general(p, q, (contract, ((), ())), preferred_element_type=F32)

    return dot(a[0], b[0]) + (dot(a[0], b[1]) + dot(a[1], b[0]))


def prepare_kernel(eps_vir, own, pairs, high, low):
    row = jnp.broadcast_to(eps_vir[...], pairs.shape)
    pairs[...] = row + row.T
    high[...], low[...] = split(own[...])


def spin(t):
    return split(2.0 * t - t.T)


def mid_kernel(e_low, e_high, pairs, low, high, *refs):
    down, up, t_mid, lh, ll, hh, hl, buf_down, buf_up, sems = refs
    half = down.shape[0]
    lh[...], ll[...] = l = split(low[...])
    hh[...], hl[...] = h = split(high[...])
    energy = e_low[0:1, 0:1] + e_high[0:1, 0:1]
    t = mm(l, h, ROWS) / (energy - pairs[...])
    turned = t.T
    s = split(2.0 * t[:half] - turned[:half])
    buf_down[...] = mm(s, h, PLAIN)
    to_down = pltpu.make_async_copy(buf_down, down, sems.at[0])
    to_down.start()
    s = split(2.0 * turned[half:] - t[half:])
    buf_up[...] = mm(s, l, PLAIN)
    to_up = pltpu.make_async_copy(buf_up, up, sems.at[1])
    to_up.start()
    t_mid[...] = t
    to_down.wait()
    to_up.wait()


def density_kernel(
    upper, e_own, e_low, e_high, pairs, t_mid, oh, ol, lh, ll, hh, hl, *refs
):
    keep, send, dens = refs
    o, l, h = (oh[...], ol[...]), (lh[...], ll[...]), (hh[...], hl[...])
    mine = e_own[0:1, 0:1]
    t = t_mid[...]
    total = mm(split(t), spin(t), ROWS)
    for other, energy in ((l, e_low), (h, e_high)):
        t = mm(o, other, ROWS) / (mine + energy[0:1, 0:1] - pairs[...])
        total = total + mm(split(t), spin(t), ROWS)
    dens[...] = total
    odd = upper[...] > 0.5
    for at in range(16):
        first = dens[at * 16 : at * 16 + 8, :]
        second = dens[at * 16 + 8 : at * 16 + 16, :]
        keep[at] = jnp.where(odd, second, first)
        send[at] = jnp.where(odd, first, second)


def near_kernel(
    e_own, e_low, e_high, pairs, oh, ol, lh, ll, hh, hl, grad, total, sem
):
    mine = e_own[0:1, 0:1]
    o, l, h = (oh[...], ol[...]), (lh[...], ll[...]), (hh[...], hl[...])
    parts = [
        spin(mm(o, other, ROWS) / (mine + energy[0:1, 0:1] - pairs[...]))
        for other, energy in ((l, e_low), (h, e_high))
    ]
    total[...] = mm(parts[0], l, PLAIN) + mm(parts[1], h, PLAIN)
    out = pltpu.make_async_copy(total, grad, sem)
    out.start()
    out.wait()


def sum_kernel(near, down0, up0, down1, up1, grad, mine, one, two, sems):
    half = down0.shape[0]
    parts, step = 4, half // 2
    copies = []
    for at in range(parts):
        rows = pl.ds(at * step, step)
        inner = pl.ds(at % 2 * step, step)
        first, second = ((down0, down1), (up0, up1))[at // 2]
        copies.append(
            (
                pltpu.make_async_copy(near.at[rows, :], mine.at[rows, :], sems.at[0, at]),
                pltpu.make_async_copy(first.at[inner, :], one.at[rows, :], sems.at[1, at]),
                pltpu.make_async_copy(second.at[inner, :], two.at[rows, :], sems.at[2, at]),
                pltpu.make_async_copy(mine.at[rows, :], grad.at[rows, :], sems.at[3, at]),
            )
        )
        for copy in copies[-1][:3]:
            copy.start()
    for at in range(parts):
        rows = slice(at * step, (at + 1) * step)
        for copy in copies[at][:3]:
            copy.wait()
        mine[rows, :] = mine[rows, :] + (one[rows, :] + two[rows, :])
        copies[at][3].start()
    for at in range(parts):
        copies[at][3].wait()


def fold_kernel(pieces, copies):
    total = pieces[0]
    for at in range(1, pieces.shape[0]):
        total = total + pieces[at]
    total = total * (1.0 / 256.0)
    for at in range(copies.shape[0]):
        copies[at] = total


def call(kernel, out, scratch, limit, flops, args, in_specs, out_specs):
    return pl.pallas_call(
        kernel,
        out_shape=tuple(
            pltpu.HBM(s, F32)
            if spec is HBM
            else jax.ShapeDtypeStruct(s, BF16 if s == (256, 1024) else F32)
            for s, spec in zip(out, out_specs)
        ),
        in_specs=in_specs,
        out_specs=out_specs,
        scratch_shapes=scratch,
        cost_estimate=pl.CostEstimate(
            flops=flops, bytes_accessed=MIB, transcendentals=0
        ),
        compiler_params=pltpu.CompilerParams(vmem_limit_bytes=limit * MIB),
    )(*args)


def in_hbm(x):
    return pltpu.with_memory_space_constraint(x, pltpu.HBM)


def body(slabs, eps_occ, eps_vir):
    own = slabs[0]
    v, n = own.shape
    low = shift(own, 1)
    high = shift(own, -1)
    tile = (8, 128)
    s_low = jnp.broadcast_to(shift(eps_occ, 1), tile)
    s_high = jnp.broadcast_to(shift(eps_occ, -1), tile)
    s_own = jnp.broadcast_to(eps_occ, tile)
    upper = jnp.broadcast_to(lax.axis_index("core").astype(F32), (8, v))
    pairs, oh, ol = call(
        prepare_kernel,
        ((v, v), (v, n), (v, n)),
        [],
        8,
        1 << 20,
        (eps_vir[None], own),
        [VMEM] * 2,
        (VMEM,) * 3,
    )
    piece = (16, 8, v)
    part = [pltpu.VMEM((v // 2, n), F32)]
    down, up, t_mid, *splits = call(
        mid_kernel,
        ((v // 2, n), (v // 2, n), (v, v)) + ((v, n),) * 4,
        part * 2 + [pltpu.SemaphoreType.DMA((2,))],
        12,
        1 << 31,
        (s_low, s_high, pairs, low, high),
        [VMEM] * 5,
        (HBM, HBM) + (VMEM,) * 5,
    )
    given = [give(down, -1, 0), give(up, 1, 0), give(down, -1, 1), give(up, 1, 1)]
    keep, send = call(
        density_kernel,
        (piece, piece),
        [pltpu.VMEM((v, v), F32)],
        12,
        1 << 31,
        (upper, s_own, s_low, s_high, pairs, t_mid, oh, ol, *splits),
        [VMEM] * 12,
        (VMEM, VMEM),
    )
    other = lax.ppermute(send, "core", [(0, 1), (1, 0)])
    parts = lax.all_to_all(
        keep + other, ("x", "far"), split_axis=0, concat_axis=0, tiled=True
    )
    (copies,) = call(fold_kernel, (piece,), [], 4, 1 << 20, (parts,), [VMEM], (VMEM,))
    copies = lax.all_to_all(
        copies, ("y", "near", "core"), split_axis=0, concat_axis=0, tiled=True
    )
    density = jnp.sum(copies.reshape(8, 16, v), axis=0)

    (near,) = call(
        near_kernel,
        ((v, n),),
        [pltpu.VMEM((v, n), F32), pltpu.SemaphoreType.DMA],
        12,
        1 << 31,
        (s_own, s_low, s_high, pairs, oh, ol, *splits),
        [VMEM] * 10,
        (HBM,),
    )
    (grad,) = call(
        sum_kernel,
        ((v, n),),
        [pltpu.VMEM((v, n), F32)] * 3 + [pltpu.SemaphoreType.DMA((4, 4))],
        8,
        1 << 20,
        (in_hbm(near), *given),
        [HBM] * 5,
        (HBM,),
    )
    return grad[None], density


def solution(mesh):
    fine = Mesh(mesh.devices.reshape(FINE_SHAPE), FINE)
    placed = (P(FINE, None, None), P(FINE), P())
    return jax.shard_map(
        body,
        mesh=fine,
        in_specs=placed,
        out_specs=(P(FINE, None, None), P(("x", "far"), None)),
        check_vma=False,
    )
```

```python
import jax
import jax.numpy as jnp
from jax import lax
from jax.experimental import pallas as pl
from jax.experimental.pallas import tpu as pltpu
from jax.sharding import Mesh, PartitionSpec as P


FINE = ("y", "near", "core", "x", "far")
FINE_SHAPE = (4, 2, 2, 4, 4)
VMEM = pl.BlockSpec(memory_space=pltpu.VMEM)
SMEM = pl.BlockSpec(memory_space=pltpu.SMEM)
HBM = pl.BlockSpec(memory_space=pltpu.HBM)
F32, BF16 = jnp.float32, jnp.bfloat16
ROWS = ((1,), (1,))
PLAIN = ((1,), (0,))
MIB = 1 << 20


def shift(value, step):
    size = lax.axis_size("far")
    return lax.ppermute(value, "far", [(i, (i + step) % size) for i in range(size)])


def give(value, step, core):
    size = lax.axis_size("far")
    pairs = [(core * size + i, core * size + (i + step) % size) for i in range(size)]
    return lax.ppermute(value, ("core", "far"), pairs)


def split(x):
    high = x.astype(BF16)
    return high, (x - high.astype(F32)).astype(BF16)


def mm(a, b, contract):
    def dot(p, q):
        return lax.dot_general(p, q, (contract, ((), ())), preferred_element_type=F32)

    return dot(a[0], b[0]) + (dot(a[0], b[1]) + dot(a[1], b[0]))


def prepare_kernel(eps_vir, own, pairs, high, low):
    row = jnp.broadcast_to(eps_vir[...], pairs.shape)
    pairs[...] = row + row.T
    high[...], low[...] = split(own[...])


def spin(t):
    return split(2.0 * t - t.T)


def mid_kernel(e_low, e_high, pairs, low, high, *refs):
    down, up, t_mid, lh, ll, hh, hl, buf_down, buf_up, sems = refs
    half = down.shape[0]
    lh[...], ll[...] = l = split(low[...])
    hh[...], hl[...] = h = split(high[...])
    energy = e_low[0:1, 0:1] + e_high[0:1, 0:1]
    t = mm(l, h, ROWS) / (energy - pairs[...])
    turned = t.T
    s = split(2.0 * t[:half] - turned[:half])
    buf_down[...] = mm(s, h, PLAIN)
    to_down = pltpu.make_async_copy(buf_down, down, sems.at[0])
    to_down.start()
    s = split(2.0 * turned[half:] - t[half:])
    buf_up[...] = mm(s, l, PLAIN)
    to_up = pltpu.make_async_copy(buf_up, up, sems.at[1])
    to_up.start()
    t_mid[...] = t
    to_down.wait()
    to_up.wait()


def density_kernel(
    upper, e_own, e_low, e_high, pairs, t_mid, oh, ol, lh, ll, hh, hl, *refs
):
    keep, send, near, dens, total, sem = refs
    o, l, h = (oh[...], ol[...]), (lh[...], ll[...]), (hh[...], hl[...])
    mine = e_own[0:1, 0:1]
    t_low = mm(o, l, ROWS) / (mine + e_low[0:1, 0:1] - pairs[...])
    t_high = mm(o, h, ROWS) / (mine + e_high[0:1, 0:1] - pairs[...])
    s_low, s_high = spin(t_low), spin(t_high)
    total[...] = mm(s_low, l, PLAIN) + mm(s_high, h, PLAIN)
    out = pltpu.make_async_copy(total, near, sem)
    out.start()
    t = t_mid[...]
    dens[...] = (
        mm(split(t), spin(t), ROWS)
        + mm(split(t_low), s_low, ROWS)
        + mm(split(t_high), s_high, ROWS)
    )
    odd = upper[...] > 0.5
    for at in range(16):
        first = dens[at * 16 : at * 16 + 8, :]
        second = dens[at * 16 + 8 : at * 16 + 16, :]
        keep[at] = jnp.where(odd, second, first)
        send[at] = jnp.where(odd, first, second)
    out.wait()


def sum_kernel(near, down0, up0, down1, up1, grad, mine, one, two, sems):
    half = down0.shape[0]
    parts, step = 4, half // 2
    copies = []
    for at in range(parts):
        rows = pl.ds(at * step, step)
        inner = pl.ds(at % 2 * step, step)
        first, second = ((down0, down1), (up0, up1))[at // 2]
        copies.append(
            (
                pltpu.make_async_copy(near.at[rows, :], mine.at[rows, :], sems.at[0, at]),
                pltpu.make_async_copy(first.at[inner, :], one.at[rows, :], sems.at[1, at]),
                pltpu.make_async_copy(second.at[inner, :], two.at[rows, :], sems.at[2, at]),
                pltpu.make_async_copy(mine.at[rows, :], grad.at[rows, :], sems.at[3, at]),
            )
        )
        for copy in copies[-1][:3]:
            copy.start()
    for at in range(parts):
        rows = slice(at * step, (at + 1) * step)
        for copy in copies[at][:3]:
            copy.wait()
        mine[rows, :] = mine[rows, :] + (one[rows, :] + two[rows, :])
        copies[at][3].start()
    for at in range(parts):
        copies[at][3].wait()


def fold_kernel(pieces, copies):
    total = pieces[0]
    for at in range(1, pieces.shape[0]):
        total = total + pieces[at]
    total = total * (1.0 / 256.0)
    for at in range(copies.shape[0]):
        copies[at] = total


def call(kernel, out, scratch, limit, flops, args, in_specs, out_specs):
    return pl.pallas_call(
        kernel,
        out_shape=tuple(
            pltpu.HBM(s, F32)
            if spec is HBM
            else jax.ShapeDtypeStruct(s, BF16 if s == (256, 1024) else F32)
            for s, spec in zip(out, out_specs)
        ),
        in_specs=in_specs,
        out_specs=out_specs,
        scratch_shapes=scratch,
        cost_estimate=pl.CostEstimate(
            flops=flops, bytes_accessed=MIB, transcendentals=0
        ),
        compiler_params=pltpu.CompilerParams(vmem_limit_bytes=limit * MIB),
    )(*args)


def in_hbm(x):
    return pltpu.with_memory_space_constraint(x, pltpu.HBM)


def body(slabs, eps_occ, eps_vir):
    own = slabs[0]
    v, n = own.shape
    low = shift(own, 1)
    high = shift(own, -1)
    tile = (8, 128)
    s_low = jnp.broadcast_to(shift(eps_occ, 1), tile)
    s_high = jnp.broadcast_to(shift(eps_occ, -1), tile)
    s_own = jnp.broadcast_to(eps_occ, tile)
    upper = jnp.broadcast_to(lax.axis_index("core").astype(F32), (8, v))
    pairs, oh, ol = call(
        prepare_kernel,
        ((v, v), (v, n), (v, n)),
        [],
        8,
        1 << 20,
        (eps_vir[None], own),
        [VMEM] * 2,
        (VMEM,) * 3,
    )
    piece = (16, 8, v)
    part = [pltpu.VMEM((v // 2, n), F32)]
    down, up, t_mid, *splits = call(
        mid_kernel,
        ((v // 2, n), (v // 2, n), (v, v)) + ((v, n),) * 4,
        part * 2 + [pltpu.SemaphoreType.DMA((2,))],
        12,
        1 << 31,
        (s_low, s_high, pairs, low, high),
        [VMEM] * 5,
        (HBM, HBM) + (VMEM,) * 5,
    )
    given = [give(down, -1, 0), give(up, 1, 0), give(down, -1, 1), give(up, 1, 1)]
    keep, send, near = call(
        density_kernel,
        (piece, piece, (v, n)),
        [
            pltpu.VMEM((v, v), F32),
            pltpu.VMEM((v, n), F32),
            pltpu.SemaphoreType.DMA,
        ],
        12,
        1 << 31,
        (upper, s_own, s_low, s_high, pairs, t_mid, oh, ol, *splits),
        [VMEM] * 12,
        (VMEM, VMEM, HBM),
    )
    other = lax.ppermute(send, "core", [(0, 1), (1, 0)])
    parts = lax.all_to_all(
        keep + other, ("x", "far"), split_axis=0, concat_axis=0, tiled=True
    )
    (copies,) = call(fold_kernel, (piece,), [], 4, 1 << 20, (parts,), [VMEM], (VMEM,))
    copies = lax.all_to_all(
        copies, ("y", "near", "core"), split_axis=0, concat_axis=0, tiled=True
    )
    density = jnp.sum(copies.reshape(8, 16, v), axis=0)

    (grad,) = call(
        sum_kernel,
        ((v, n),),
        [pltpu.VMEM((v, n), F32)] * 3 + [pltpu.SemaphoreType.DMA((4, 4))],
        8,
        1 << 20,
        (in_hbm(near), *given),
        [HBM] * 5,
        (HBM,),
    )
    return grad[None], density


def solution(mesh):
    fine = Mesh(mesh.devices.reshape(FINE_SHAPE), FINE)
    placed = (P(FINE, None, None), P(FINE), P())
    return jax.shard_map(
        body,
        mesh=fine,
        in_specs=placed,
        out_specs=(P(FINE, None, None), P(("x", "far"), None)),
        check_vma=False,
    )
```

```python
import jax
import jax.numpy as jnp
from jax import lax
from jax.experimental import pallas as pl
from jax.experimental.pallas import tpu as pltpu
from jax.sharding import Mesh, PartitionSpec as P


FINE = ("y", "near", "core", "x", "far")
FINE_SHAPE = (4, 2, 2, 4, 4)
VMEM = pl.BlockSpec(memory_space=pltpu.VMEM)
SMEM = pl.BlockSpec(memory_space=pltpu.SMEM)
HBM = pl.BlockSpec(memory_space=pltpu.HBM)
F32, BF16 = jnp.float32, jnp.bfloat16
ROWS = ((1,), (1,))
PLAIN = ((1,), (0,))
MIB = 1 << 20


def shift(value, step):
    size = lax.axis_size("far")
    return lax.ppermute(value, "far", [(i, (i + step) % size) for i in range(size)])


def split(x):
    high = x.astype(BF16)
    return high, (x - high.astype(F32)).astype(BF16)


def mm(a, b, contract):
    def dot(p, q):
        return lax.dot_general(p, q, (contract, ((), ())), preferred_element_type=F32)

    return dot(a[0], b[0]) + (dot(a[0], b[1]) + dot(a[1], b[0]))


def prepare_kernel(eps_vir, own, pairs, high, low):
    row = jnp.broadcast_to(eps_vir[...], pairs.shape)
    pairs[...] = row + row.T
    high[...], low[...] = split(own[...])


def spin(t):
    return split(2.0 * t - t.T)


def fill(first, second, high, low):
    half = first.shape[0]
    high[:half, :], low[:half, :] = split(first[...])
    high[half:, :], low[half:, :] = split(second[...])
    return high[...], low[...]


def density_kernel(upper, e_own, e_low, e_high, pairs, oh, ol, *refs):
    low_a, low_b, high_a, high_b, keep, send, near = refs[:7]
    lh, ll, hh, hl, dens, total, sem = refs[7:]
    o = (oh[...], ol[...])
    l, h = fill(low_a, low_b, lh, ll), fill(high_a, high_b, hh, hl)
    mine, below, above = e_own[0:1, 0:1], e_low[0:1, 0:1], e_high[0:1, 0:1]
    t_low = mm(o, l, ROWS) / (mine + below - pairs[...])
    t_high = mm(o, h, ROWS) / (mine + above - pairs[...])
    s_low, s_high = spin(t_low), spin(t_high)
    total[...] = mm(s_low, l, PLAIN) + mm(s_high, h, PLAIN)
    out = pltpu.make_async_copy(total, near, sem)
    out.start()
    t = mm(l, h, ROWS) / (below + above - pairs[...])
    dens[...] = (
        mm(split(t), spin(t), ROWS)
        + mm(split(t_low), s_low, ROWS)
        + mm(split(t_high), s_high, ROWS)
    )
    odd = upper[...] > 0.5
    for at in range(16):
        first = dens[at * 16 : at * 16 + 8, :]
        second = dens[at * 16 + 8 : at * 16 + 16, :]
        keep[at] = jnp.where(odd, second, first)
        send[at] = jnp.where(odd, first, second)
    out.wait()


def far_kernel(e_own, e_far, pairs, oh, ol, far_a, far_b, near, grad, *scratch):
    fh, fl, before, total, sem_in, sem_out = scratch
    fetch = pltpu.make_async_copy(near, before, sem_in)
    fetch.start()
    f = fill(far_a, far_b, fh, fl)
    energy = e_own[0:1, 0:1] + e_far[0:1, 0:1]
    s = spin(mm((oh[...], ol[...]), f, ROWS) / (energy - pairs[...]))
    fetch.wait()
    blocks = 4
    width = total.shape[1] // blocks
    outs = []
    for at in range(blocks):
        cols = slice(at * width, (at + 1) * width)
        total[:, cols] = before[:, cols] + mm(s, (f[0][:, cols], f[1][:, cols]), PLAIN)
        outs.append(
            pltpu.make_async_copy(
                total.at[:, cols], grad.at[:, cols], sem_out.at[at]
            )
        )
        outs[-1].start()
    for out in outs:
        out.wait()


def fold_kernel(pieces, copies):
    total = pieces[0]
    for at in range(1, pieces.shape[0]):
        total = total + pieces[at]
    total = total * (1.0 / 256.0)
    for at in range(copies.shape[0]):
        copies[at] = total


def call(kernel, out, scratch, limit, flops, args, in_specs, out_specs):
    return pl.pallas_call(
        kernel,
        out_shape=tuple(
            pltpu.HBM(s, F32)
            if spec is HBM
            else jax.ShapeDtypeStruct(s, BF16 if s == (256, 1024) else F32)
            for s, spec in zip(out, out_specs)
        ),
        in_specs=in_specs,
        out_specs=out_specs,
        scratch_shapes=scratch,
        cost_estimate=pl.CostEstimate(
            flops=flops, bytes_accessed=MIB, transcendentals=0
        ),
        compiler_params=pltpu.CompilerParams(vmem_limit_bytes=limit * MIB),
    )(*args)


def in_hbm(x):
    return pltpu.with_memory_space_constraint(x, pltpu.HBM)


def body(slabs, eps_occ, eps_vir):
    own = slabs[0]
    v, n = own.shape
    mid = v // 2
    own_a, own_b = own[:mid], own[mid:]
    low_a = shift(own_a, 1)
    high_b = shift(own_b, -1)
    tile = (8, 128)
    e_low = shift(eps_occ, 1)
    e_high = shift(eps_occ, -1)
    e_far = shift(eps_occ, 2)
    s_low, s_high, s_far, s_own = (
        jnp.broadcast_to(e, tile) for e in (e_low, e_high, e_far, eps_occ)
    )
    slabs = (low_a, shift(own_b, 1), shift(own_a, -1), high_b)
    far_a = shift(low_a, 1)
    far_b = shift(high_b, -1)
    upper = jnp.broadcast_to(lax.axis_index("core").astype(F32), (8, v))
    pairs, oh, ol = call(
        prepare_kernel,
        ((v, v), (v, n), (v, n)),
        [],
        8,
        1 << 20,
        (eps_vir[None], own),
        [VMEM] * 2,
        (VMEM,) * 3,
    )
    piece = (16, 8, v)
    wide, full = pltpu.VMEM((v, n), BF16), pltpu.VMEM((v, n), F32)
    keep, send, near = call(
        density_kernel,
        (piece, piece, (v, n)),
        [wide] * 4 + [pltpu.VMEM((v, v), F32), full, pltpu.SemaphoreType.DMA],
        14,
        1 << 31,
        (upper, s_own, s_low, s_high, pairs, oh, ol, *slabs),
        [VMEM] * 11,
        (VMEM, VMEM, HBM),
    )
    other = lax.ppermute(send, "core", [(0, 1), (1, 0)])
    parts = lax.all_to_all(
        keep + other, ("x", "far"), split_axis=0, concat_axis=0, tiled=True
    )
    (copies,) = call(fold_kernel, (piece,), [], 4, 1 << 20, (parts,), [VMEM], (VMEM,))
    copies = lax.all_to_all(
        copies, ("y", "near", "core"), split_axis=0, concat_axis=0, tiled=True
    )
    density = jnp.sum(copies.reshape(8, 16, v), axis=0)

    (grad,) = call(
        far_kernel,
        ((v, n),),
        [wide] * 2
        + [full] * 2
        + [pltpu.SemaphoreType.DMA, pltpu.SemaphoreType.DMA((4,))],
        12,
        1 << 31,
        (s_own, s_far, pairs, oh, ol, far_a, far_b, in_hbm(near)),
        [VMEM] * 7 + [HBM],
        (HBM,),
    )
    return grad[None], density


def solution(mesh):
    fine = Mesh(mesh.devices.reshape(FINE_SHAPE), FINE)
    placed = (P(FINE, None, None), P(FINE), P())
    return jax.shard_map(
        body,
        mesh=fine,
        in_specs=placed,
        out_specs=(P(FINE, None, None), P(("x", "far"), None)),
        check_vma=False,
    )
```

```python
import jax
import jax.numpy as jnp
from jax import lax
from jax.experimental import pallas as pl
from jax.experimental.pallas import tpu as pltpu
from jax.sharding import Mesh, PartitionSpec as P


FINE = ("y", "near", "core", "x", "far")
FINE_SHAPE = (4, 2, 2, 4, 4)
VMEM = pl.BlockSpec(memory_space=pltpu.VMEM)
SMEM = pl.BlockSpec(memory_space=pltpu.SMEM)
HBM = pl.BlockSpec(memory_space=pltpu.HBM)
F32, BF16 = jnp.float32, jnp.bfloat16
ROWS = ((1,), (1,))
PLAIN = ((1,), (0,))
MIB = 1 << 20


def role_shift(value, step):
    size = lax.axis_size("far")
    pairs = []
    for core, way in ((0, step), (1, -step)):
        base = core * size
        pairs += [(base + i, base + (i + way) % size) for i in range(size)]
    return lax.ppermute(value, ("core", "far"), pairs)


def split(x):
    high = x.astype(BF16)
    return high, (x - high.astype(F32)).astype(BF16)


def mm(a, b, contract):
    def dot(p, q):
        return lax.dot_general(p, q, (contract, ((), ())), preferred_element_type=F32)

    return dot(a[0], b[0]) + (dot(a[0], b[1]) + dot(a[1], b[0]))


def prepare_kernel(eps_vir, own, pairs, high, low):
    row = jnp.broadcast_to(eps_vir[...], pairs.shape)
    pairs[...] = row + row.T
    high[...], low[...] = split(own[...])


def spin(t):
    return split(2.0 * t - t.T)


def pair_kernel(upper, e_own, e_one, e_two, pairs, oh, ol, one, two, *refs):
    keep, send, gift, near, buf, total, dens, sems = refs
    o, a, b = (oh[...], ol[...]), split(one[...]), split(two[...])
    mine, first, second = e_own[0:1, 0:1], e_one[0:1, 0:1], e_two[0:1, 0:1]
    t = mm(b, a, ROWS) / (first + second - pairs[...])
    s = spin(t)
    buf[...] = mm(s, a, PLAIN)
    out = [pltpu.make_async_copy(buf, gift, sems.at[0])]
    out[0].start()
    t_one = mm(o, a, ROWS) / (mine + first - pairs[...])
    t_two = mm(o, b, ROWS) / (mine + second - pairs[...])
    s_one, s_two = spin(t_one), spin(t_two)
    total[...] = mm(s_one, a, PLAIN) + mm(s_two, b, PLAIN)
    out.append(pltpu.make_async_copy(total, near, sems.at[1]))
    out[1].start()
    dens[...] = (
        mm(split(t), s, ROWS)
        + mm(split(t_one), s_one, ROWS)
        + mm(split(t_two), s_two, ROWS)
    )
    odd = upper[...] > 0.5
    for at in range(16):
        low = dens[at * 16 : at * 16 + 8, :]
        high = dens[at * 16 + 8 : at * 16 + 16, :]
        keep[at] = jnp.where(odd, high, low)
        send[at] = jnp.where(odd, low, high)
    for copy in out:
        copy.wait()


def join_kernel(keep, other, copies):
    for at in range(copies.shape[1]):
        piece = keep[at] + other[at]
        for copy in range(copies.shape[0]):
            copies[copy, at] = piece


def sum_kernel(near, gift, grad, mine, other, sems):
    parts = 4
    step = mine.shape[0] // parts
    copies = []
    for at in range(parts):
        rows = pl.ds(at * step, step)
        copies.append(
            (
                pltpu.make_async_copy(near.at[rows, :], mine.at[rows, :], sems.at[0, at]),
                pltpu.make_async_copy(gift.at[rows, :], other.at[rows, :], sems.at[1, at]),
                pltpu.make_async_copy(mine.at[rows, :], grad.at[rows, :], sems.at[2, at]),
            )
        )
        copies[-1][0].start()
        copies[-1][1].start()
    for at in range(parts):
        rows = slice(at * step, (at + 1) * step)
        copies[at][0].wait()
        copies[at][1].wait()
        mine[rows, :] = mine[rows, :] + other[rows, :]
        copies[at][2].start()
    for at in range(parts):
        copies[at][2].wait()


def fold_kernel(pieces, copies):
    total = pieces[0]
    for at in range(1, pieces.shape[0]):
        total = total + pieces[at]
    total = total * (1.0 / 256.0)
    for at in range(copies.shape[0]):
        row = at // 2 % 4 * 8
        copies[at] = total[row : row + 8, :]


def call(kernel, out, scratch, limit, flops, args, in_specs, out_specs):
    return pl.pallas_call(
        kernel,
        out_shape=tuple(
            pltpu.HBM(s, F32)
            if spec is HBM
            else jax.ShapeDtypeStruct(s, BF16 if s == (256, 1024) else F32)
            for s, spec in zip(out, out_specs)
        ),
        in_specs=in_specs,
        out_specs=out_specs,
        scratch_shapes=scratch,
        cost_estimate=pl.CostEstimate(
            flops=flops, bytes_accessed=MIB, transcendentals=0
        ),
        compiler_params=pltpu.CompilerParams(vmem_limit_bytes=limit * MIB),
    )(*args)


def in_hbm(x):
    return pltpu.with_memory_space_constraint(x, pltpu.HBM)


def body(slabs, eps_occ, eps_vir):
    own = slabs[0]
    v, n = own.shape
    one = role_shift(own, 1)
    two = role_shift(own, -1)
    e_one = role_shift(eps_occ, 1)
    e_two = role_shift(eps_occ, -1)
    tile = (8, 128)
    s_one, s_two, s_own = (jnp.broadcast_to(e, tile) for e in (e_one, e_two, eps_occ))
    upper = jnp.broadcast_to(lax.axis_index("core").astype(F32), (8, v))
    pairs, oh, ol = call(
        prepare_kernel,
        ((v, v), (v, n), (v, n)),
        [],
        8,
        1 << 20,
        (eps_vir[None], own),
        [VMEM] * 2,
        (VMEM,) * 3,
    )
    piece = (16, 8, v)
    full = pltpu.VMEM((v, n), F32)
    keep, send, gift, near = call(
        pair_kernel,
        (piece, piece, (v, n), (v, n)),
        [full] * 2 + [pltpu.VMEM((v, v), F32), pltpu.SemaphoreType.DMA((2,))],
        14,
        1 << 31,
        (upper, s_own, s_one, s_two, pairs, oh, ol, one, two),
        [VMEM] * 9,
        (VMEM, VMEM, HBM, HBM),
    )
    other = lax.ppermute(send, "core", [(0, 1), (1, 0)])
    gift = role_shift(gift, 1)
    (mine,) = call(
        join_kernel, ((4,) + piece,), [], 4, 1 << 20, (keep, other), [VMEM] * 2, (VMEM,)
    )
    parts = lax.all_to_all(
        mine.reshape(16, 32, v), ("y", "x"), split_axis=0, concat_axis=0, tiled=True
    )
    (copies,) = call(fold_kernel, (piece,), [], 4, 1 << 20, (parts,), [VMEM], (VMEM,))
    copies = lax.all_to_all(
        copies, ("near", "far", "core"), split_axis=0, concat_axis=0, tiled=True
    )
    density = jnp.sum(copies.reshape(8, 16, v), axis=0)
    (grad,) = call(
        sum_kernel,
        ((v, n),),
        [full] * 2 + [pltpu.SemaphoreType.DMA((3, 4))],
        8,
        1 << 20,
        (in_hbm(near), gift),
        [HBM] * 2,
        (HBM,),
    )
    return grad[None], density


def solution(mesh):
    fine = Mesh(mesh.devices.reshape(FINE_SHAPE), FINE)
    placed = (P(FINE, None, None), P(FINE), P())
    return jax.shard_map(
        body,
        mesh=fine,
        in_specs=placed,
        out_specs=(P(FINE, None, None), P(("x", "far"), None)),
        check_vma=False,
    )
```

```python
import jax
import jax.numpy as jnp
from jax import lax
from jax.experimental import pallas as pl
from jax.experimental.pallas import tpu as pltpu
from jax.sharding import Mesh, PartitionSpec as P


FINE = ("y", "near", "core", "x", "far")
FINE_SHAPE = (4, 2, 2, 4, 4)
VMEM = pl.BlockSpec(memory_space=pltpu.VMEM)
SMEM = pl.BlockSpec(memory_space=pltpu.SMEM)
HBM = pl.BlockSpec(memory_space=pltpu.HBM)
F32, BF16 = jnp.float32, jnp.bfloat16
ROWS = ((1,), (1,))
PLAIN = ((1,), (0,))
MIB = 1 << 20


def role_shift(value, step):
    size = lax.axis_size("far")
    pairs = []
    for core, way in ((0, step), (1, -step)):
        base = core * size
        pairs += [(base + i, base + (i + way) % size) for i in range(size)]
    return lax.ppermute(value, ("core", "far"), pairs)


def split(x):
    high = x.astype(BF16)
    return high, (x - high.astype(F32)).astype(BF16)


def mm(a, b, contract):
    def dot(p, q):
        return lax.dot_general(p, q, (contract, ((), ())), preferred_element_type=F32)

    return dot(a[0], b[0]) + (dot(a[0], b[1]) + dot(a[1], b[0]))


def prepare_kernel(eps_vir, own, pairs, high, low):
    row = jnp.broadcast_to(eps_vir[...], pairs.shape)
    pairs[...] = row + row.T
    high[...], low[...] = split(own[...])


def spin(t):
    return split(2.0 * t - t.T)


def gift_kernel(e_one, e_two, pairs, one, two, *refs):
    gift, t_mid, ah, al, bh, bl, buf, sem = refs
    ah[...], al[...] = a = split(one[...])
    bh[...], bl[...] = b = split(two[...])
    t = mm(b, a, ROWS) / (e_one[0:1, 0:1] + e_two[0:1, 0:1] - pairs[...])
    buf[...] = mm(spin(t), a, PLAIN)
    out = pltpu.make_async_copy(buf, gift, sem)
    out.start()
    t_mid[...] = t
    out.wait()


def density_kernel(upper, e_own, e_one, e_two, pairs, oh, ol, t_mid, *refs):
    ah, al, bh, bl, keep, send, near, total, dens, sem = refs
    o, a, b = (oh[...], ol[...]), (ah[...], al[...]), (bh[...], bl[...])
    mine, first, second = e_own[0:1, 0:1], e_one[0:1, 0:1], e_two[0:1, 0:1]
    t_one = mm(o, a, ROWS) / (mine + first - pairs[...])
    t_two = mm(o, b, ROWS) / (mine + second - pairs[...])
    s_one, s_two = spin(t_one), spin(t_two)
    total[...] = mm(s_one, a, PLAIN) + mm(s_two, b, PLAIN)
    out = pltpu.make_async_copy(total, near, sem)
    out.start()
    t = t_mid[...]
    dens[...] = (
        mm(split(t), spin(t), ROWS)
        + mm(split(t_one), s_one, ROWS)
        + mm(split(t_two), s_two, ROWS)
    )
    odd = upper[...] > 0.5
    for at in range(16):
        low = dens[at * 16 : at * 16 + 8, :]
        high = dens[at * 16 + 8 : at * 16 + 16, :]
        keep[at] = jnp.where(odd, high, low)
        send[at] = jnp.where(odd, low, high)
    out.wait()


def join_kernel(keep, other, copies):
    for at in range(copies.shape[1]):
        piece = keep[at] + other[at]
        for copy in range(copies.shape[0]):
            copies[copy, at] = piece


def sum_kernel(near, gift, grad, mine, other, sems):
    parts = 4
    step = mine.shape[0] // parts
    copies = []
    for at in range(parts):
        rows = pl.ds(at * step, step)
        copies.append(
            (
                pltpu.make_async_copy(near.at[rows, :], mine.at[rows, :], sems.at[0, at]),
                pltpu.make_async_copy(gift.at[rows, :], other.at[rows, :], sems.at[1, at]),
                pltpu.make_async_copy(mine.at[rows, :], grad.at[rows, :], sems.at[2, at]),
            )
        )
        copies[-1][0].start()
        copies[-1][1].start()
    for at in range(parts):
        rows = slice(at * step, (at + 1) * step)
        copies[at][0].wait()
        copies[at][1].wait()
        mine[rows, :] = mine[rows, :] + other[rows, :]
        copies[at][2].start()
    for at in range(parts):
        copies[at][2].wait()


def fold_kernel(pieces, copies):
    total = pieces[0]
    for at in range(1, pieces.shape[0]):
        total = total + pieces[at]
    total = total * (1.0 / 256.0)
    for at in range(copies.shape[0]):
        row = at // 2 % 4 * 8
        copies[at] = total[row : row + 8, :]


def call(kernel, out, scratch, limit, flops, args, in_specs, out_specs):
    return pl.pallas_call(
        kernel,
        out_shape=tuple(
            pltpu.HBM(s, F32)
            if spec is HBM
            else jax.ShapeDtypeStruct(s, BF16 if s == (256, 1024) else F32)
            for s, spec in zip(out, out_specs)
        ),
        in_specs=in_specs,
        out_specs=out_specs,
        scratch_shapes=scratch,
        cost_estimate=pl.CostEstimate(
            flops=flops, bytes_accessed=MIB, transcendentals=0
        ),
        compiler_params=pltpu.CompilerParams(vmem_limit_bytes=limit * MIB),
    )(*args)


def in_hbm(x):
    return pltpu.with_memory_space_constraint(x, pltpu.HBM)


def body(slabs, eps_occ, eps_vir):
    own = slabs[0]
    v, n = own.shape
    one = role_shift(own, 1)
    two = role_shift(own, -1)
    e_one = role_shift(eps_occ, 1)
    e_two = role_shift(eps_occ, -1)
    tile = (8, 128)
    s_one, s_two, s_own = (jnp.broadcast_to(e, tile) for e in (e_one, e_two, eps_occ))
    upper = jnp.broadcast_to(lax.axis_index("core").astype(F32), (8, v))
    pairs, oh, ol = call(
        prepare_kernel,
        ((v, v), (v, n), (v, n)),
        [],
        8,
        1 << 20,
        (eps_vir[None], own),
        [VMEM] * 2,
        (VMEM,) * 3,
    )
    piece = (16, 8, v)
    full = pltpu.VMEM((v, n), F32)
    gift, t_mid, *splits = call(
        gift_kernel,
        ((v, n), (v, v)) + ((v, n),) * 4,
        [full, pltpu.SemaphoreType.DMA],
        12,
        1 << 31,
        (s_one, s_two, pairs, one, two),
        [VMEM] * 5,
        (HBM,) + (VMEM,) * 5,
    )
    gift = role_shift(gift, 1)
    keep, send, near = call(
        density_kernel,
        (piece, piece, (v, n)),
        [full, pltpu.VMEM((v, v), F32), pltpu.SemaphoreType.DMA],
        12,
        1 << 31,
        (upper, s_own, s_one, s_two, pairs, oh, ol, t_mid, *splits),
        [VMEM] * 12,
        (VMEM, VMEM, HBM),
    )
    other = lax.ppermute(send, "core", [(0, 1), (1, 0)])
    (mine,) = call(
        join_kernel, ((4,) + piece,), [], 4, 1 << 20, (keep, other), [VMEM] * 2, (VMEM,)
    )
    parts = lax.all_to_all(
        mine.reshape(16, 32, v), ("y", "x"), split_axis=0, concat_axis=0, tiled=True
    )
    (copies,) = call(fold_kernel, (piece,), [], 4, 1 << 20, (parts,), [VMEM], (VMEM,))
    copies = lax.all_to_all(
        copies, ("near", "far", "core"), split_axis=0, concat_axis=0, tiled=True
    )
    density = jnp.sum(copies.reshape(8, 16, v), axis=0)
    (grad,) = call(
        sum_kernel,
        ((v, n),),
        [full] * 2 + [pltpu.SemaphoreType.DMA((3, 4))],
        8,
        1 << 20,
        (in_hbm(near), gift),
        [HBM] * 2,
        (HBM,),
    )
    return grad[None], density


def solution(mesh):
    fine = Mesh(mesh.devices.reshape(FINE_SHAPE), FINE)
    placed = (P(FINE, None, None), P(FINE), P())
    return jax.shard_map(
        body,
        mesh=fine,
        in_specs=placed,
        out_specs=(P(FINE, None, None), P(("x", "far"), None)),
        check_vma=False,
    )
```

```python
import jax
import jax.numpy as jnp
from jax import lax
from jax.experimental import pallas as pl
from jax.experimental.pallas import tpu as pltpu
from jax.sharding import Mesh, PartitionSpec as P


FINE = ("y", "near", "core", "x", "far")
FINE_SHAPE = (4, 2, 2, 4, 4)
VMEM = pl.BlockSpec(memory_space=pltpu.VMEM)
SMEM = pl.BlockSpec(memory_space=pltpu.SMEM)
HBM = pl.BlockSpec(memory_space=pltpu.HBM)
F32, BF16 = jnp.float32, jnp.bfloat16
ROWS = ((1,), (1,))
PLAIN = ((1,), (0,))
MIB = 1 << 20
EARLY = 128


def role_shift(value, step):
    size = lax.axis_size("far")
    pairs = []
    for near, way in ((0, -step), (1, step)):
        base = near * size
        pairs += [(base + i, base + (i + way) % size) for i in range(size)]
    return lax.ppermute(value, ("near", "far"), pairs)


def split(x):
    high = x.astype(BF16)
    return high, (x - high.astype(F32)).astype(BF16)


def mm(a, b, contract):
    def dot(p, q):
        return lax.dot_general(p, q, (contract, ((), ())), preferred_element_type=F32)

    return dot(a[0], b[0]) + (dot(a[0], b[1]) + dot(a[1], b[0]))


def prepare_kernel(eps_vir, own, pairs, high, low):
    row = jnp.broadcast_to(eps_vir[...], pairs.shape)
    pairs[...] = row + row.T
    high[...], low[...] = split(own[...])


def spin(t):
    return split(2.0 * t - t.T)


def pair_kernel(upper, e_own, e_one, e_two, pairs, oh, ol, one, two, *refs):
    keep, send, gift, later, near, buf, total, dens, sems = refs
    o, a, b = (oh[...], ol[...]), split(one[...]), split(two[...])
    mine, first, second = e_own[0:1, 0:1], e_one[0:1, 0:1], e_two[0:1, 0:1]
    t = mm(b, a, ROWS) / (first + second - pairs[...])
    s = spin(t)
    buf[...] = mm(s, a, PLAIN)
    out = [
        pltpu.make_async_copy(buf.at[:EARLY, :], gift, sems.at[0]),
        pltpu.make_async_copy(buf.at[EARLY:, :], later, sems.at[2]),
    ]
    for copy in out:
        copy.start()
    t_one = mm(o, a, ROWS) / (mine + first - pairs[...])
    t_two = mm(o, b, ROWS) / (mine + second - pairs[...])
    s_one, s_two = spin(t_one), spin(t_two)
    total[...] = mm(s_one, a, PLAIN) + mm(s_two, b, PLAIN)
    out.append(pltpu.make_async_copy(total, near, sems.at[1]))
    out[2].start()
    dens[...] = (
        mm(split(t), s, ROWS)
        + mm(split(t_one), s_one, ROWS)
        + mm(split(t_two), s_two, ROWS)
    )
    odd = upper[...] > 0.5
    for at in range(16):
        low = dens[at * 16 : at * 16 + 8, :]
        high = dens[at * 16 + 8 : at * 16 + 16, :]
        keep[at] = jnp.where(odd, high, low)
        send[at] = jnp.where(odd, low, high)
    for copy in out:
        copy.wait()


def sum_kernel(near, gift, later, grad, mine, other, sems):
    cuts = ((0, EARLY), (EARLY, EARLY + 64), (EARLY + 64, mine.shape[0]))
    copies = []
    for at, (low, high) in enumerate(cuts):
        rows = pl.ds(low, high - low)
        source = gift if at == 0 else later.at[pl.ds(low - EARLY, high - low), :]
        copies.append(
            (
                pltpu.make_async_copy(near.at[rows, :], mine.at[rows, :], sems.at[0, at]),
                pltpu.make_async_copy(source, other.at[rows, :], sems.at[1, at]),
                pltpu.make_async_copy(mine.at[rows, :], grad.at[rows, :], sems.at[2, at]),
            )
        )
        copies[-1][0].start()
        copies[-1][1].start()
    for at, (low, high) in enumerate(cuts):
        copies[at][0].wait()
        copies[at][1].wait()
        mine[low:high, :] = mine[low:high, :] + other[low:high, :]
        copies[at][2].start()
    for copy in copies:
        copy[2].wait()


def fold_kernel(pieces, copies):
    total = pieces[0]
    for at in range(1, pieces.shape[0]):
        total = total + pieces[at]
    total = total * (1.0 / 256.0)
    for at in range(copies.shape[0]):
        copies[at] = total


def call(kernel, out, scratch, limit, flops, args, in_specs, out_specs):
    return pl.pallas_call(
        kernel,
        out_shape=tuple(
            pltpu.HBM(s, F32)
            if spec is HBM
            else jax.ShapeDtypeStruct(s, BF16 if s == (256, 1024) else F32)
            for s, spec in zip(out, out_specs)
        ),
        in_specs=in_specs,
        out_specs=out_specs,
        scratch_shapes=scratch,
        cost_estimate=pl.CostEstimate(
            flops=flops, bytes_accessed=MIB, transcendentals=0
        ),
        compiler_params=pltpu.CompilerParams(vmem_limit_bytes=limit * MIB),
    )(*args)


def in_hbm(x):
    return pltpu.with_memory_space_constraint(x, pltpu.HBM)


def body(slabs, eps_occ, eps_vir):
    own = slabs[0]
    v, n = own.shape
    one = role_shift(own, 1)
    two = role_shift(own, -1)
    e_one = role_shift(eps_occ, 1)
    e_two = role_shift(eps_occ, -1)
    tile = (8, 128)
    s_one, s_two, s_own = (jnp.broadcast_to(e, tile) for e in (e_one, e_two, eps_occ))
    upper = jnp.broadcast_to(lax.axis_index("core").astype(F32), (8, v))
    pairs, oh, ol = call(
        prepare_kernel,
        ((v, v), (v, n), (v, n)),
        [],
        8,
        1 << 20,
        (eps_vir[None], own),
        [VMEM] * 2,
        (VMEM,) * 3,
    )
    piece = (16, 8, v)
    full = pltpu.VMEM((v, n), F32)
    keep, send, gift, later, near = call(
        pair_kernel,
        (piece, piece, (EARLY, n), (v - EARLY, n), (v, n)),
        [full] * 2 + [pltpu.VMEM((v, v), F32), pltpu.SemaphoreType.DMA((3,))],
        14,
        1 << 31,
        (upper, s_own, s_one, s_two, pairs, oh, ol, one, two),
        [VMEM] * 9,
        (VMEM, VMEM, HBM, HBM, HBM),
    )
    other = lax.ppermute(send, "core", [(0, 1), (1, 0)])
    gift = role_shift(gift, 1)
    later = role_shift(later, 1)
    parts = lax.all_to_all(
        keep + other, ("x", "far"), split_axis=0, concat_axis=0, tiled=True
    )
    (copies,) = call(fold_kernel, (piece,), [], 4, 1 << 20, (parts,), [VMEM], (VMEM,))
    copies = lax.all_to_all(
        copies, ("y", "near", "core"), split_axis=0, concat_axis=0, tiled=True
    )
    density = jnp.sum(copies.reshape(8, 16, v), axis=0)
    (grad,) = call(
        sum_kernel,
        ((v, n),),
        [full] * 2 + [pltpu.SemaphoreType.DMA((3, 3))],
        8,
        1 << 20,
        (in_hbm(near), gift, later),
        [HBM] * 3,
        (HBM,),
    )
    return grad[None], density


def solution(mesh):
    fine = Mesh(mesh.devices.reshape(FINE_SHAPE), FINE)
    placed = (P(FINE, None, None), P(FINE), P())
    return jax.shard_map(
        body,
        mesh=fine,
        in_specs=placed,
        out_specs=(P(FINE, None, None), P(("x", "far"), None)),
        check_vma=False,
    )
```

```python
import jax
import jax.numpy as jnp
from jax import lax
from jax.experimental import pallas as pl
from jax.experimental.pallas import tpu as pltpu
from jax.sharding import Mesh, PartitionSpec as P


FINE = ("y", "near", "core", "x", "far")
FINE_SHAPE = (4, 2, 2, 4, 4)
VMEM = pl.BlockSpec(memory_space=pltpu.VMEM)
SMEM = pl.BlockSpec(memory_space=pltpu.SMEM)
HBM = pl.BlockSpec(memory_space=pltpu.HBM)
F32, BF16 = jnp.float32, jnp.bfloat16
ROWS = ((1,), (1,))
PLAIN = ((1,), (0,))
MIB = 1 << 20
EARLY = 128


def role_shift(value, step):
    size = lax.axis_size("far")
    pairs = []
    for core, way in ((0, step), (1, -step)):
        base = core * size
        pairs += [(base + i, base + (i + way) % size) for i in range(size)]
    return lax.ppermute(value, ("core", "far"), pairs)


def split(x):
    high = x.astype(BF16)
    return high, (x - high.astype(F32)).astype(BF16)


def mm(a, b, contract):
    def dot(p, q):
        return lax.dot_general(p, q, (contract, ((), ())), preferred_element_type=F32)

    return dot(a[0], b[0]) + (dot(a[0], b[1]) + dot(a[1], b[0]))


def prepare_kernel(eps_vir, own, pairs, high, low):
    row = jnp.broadcast_to(eps_vir[...], pairs.shape)
    pairs[...] = row + row.T
    high[...], low[...] = split(own[...])


def spin(t):
    return split(2.0 * t - t.T)


def pair_kernel(upper, e_own, e_one, e_two, pairs, oh, ol, one, two, *refs):
    keep, send, gift, later, near, buf, total, dens, sems = refs
    o, a, b = (oh[...], ol[...]), split(one[...]), split(two[...])
    mine, first, second = e_own[0:1, 0:1], e_one[0:1, 0:1], e_two[0:1, 0:1]
    t = mm(b, a, ROWS) / (first + second - pairs[...])
    s = spin(t)
    buf[...] = mm(s, a, PLAIN)
    out = [
        pltpu.make_async_copy(buf.at[:EARLY, :], gift, sems.at[0]),
        pltpu.make_async_copy(buf.at[EARLY:, :], later, sems.at[2]),
    ]
    for copy in out:
        copy.start()
    t_one = mm(o, a, ROWS) / (mine + first - pairs[...])
    t_two = mm(o, b, ROWS) / (mine + second - pairs[...])
    s_one, s_two = spin(t_one), spin(t_two)
    total[...] = mm(s_one, a, PLAIN) + mm(s_two, b, PLAIN)
    out.append(pltpu.make_async_copy(total, near, sems.at[1]))
    out[2].start()
    dens[...] = (
        mm(split(t), s, ROWS)
        + mm(split(t_one), s_one, ROWS)
        + mm(split(t_two), s_two, ROWS)
    )
    odd = upper[...] > 0.5
    for at in range(16):
        low = dens[at * 16 : at * 16 + 8, :]
        high = dens[at * 16 + 8 : at * 16 + 16, :]
        keep[at] = jnp.where(odd, high, low)
        send[at] = jnp.where(odd, low, high)
    for copy in out:
        copy.wait()


def sum_kernel(near, gift, later, grad, mine, other, sems):
    cuts = ((0, EARLY), (EARLY, EARLY + 64), (EARLY + 64, mine.shape[0]))
    copies = []
    for at, (low, high) in enumerate(cuts):
        rows = pl.ds(low, high - low)
        source = gift if at == 0 else later.at[pl.ds(low - EARLY, high - low), :]
        copies.append(
            (
                pltpu.make_async_copy(near.at[rows, :], mine.at[rows, :], sems.at[0, at]),
                pltpu.make_async_copy(source, other.at[rows, :], sems.at[1, at]),
                pltpu.make_async_copy(mine.at[rows, :], grad.at[rows, :], sems.at[2, at]),
            )
        )
        copies[-1][0].start()
        copies[-1][1].start()
    for at, (low, high) in enumerate(cuts):
        copies[at][0].wait()
        copies[at][1].wait()
        mine[low:high, :] = mine[low:high, :] + other[low:high, :]
        copies[at][2].start()
    for copy in copies:
        copy[2].wait()


def fold_kernel(pieces, copies):
    total = pieces[0]
    for at in range(1, pieces.shape[0]):
        total = total + pieces[at]
    total = total * (1.0 / 256.0)
    for at in range(copies.shape[0]):
        copies[at] = total


def call(kernel, out, scratch, limit, flops, args, in_specs, out_specs):
    return pl.pallas_call(
        kernel,
        out_shape=tuple(
            pltpu.HBM(s, F32)
            if spec is HBM
            else jax.ShapeDtypeStruct(s, BF16 if s == (256, 1024) else F32)
            for s, spec in zip(out, out_specs)
        ),
        in_specs=in_specs,
        out_specs=out_specs,
        scratch_shapes=scratch,
        cost_estimate=pl.CostEstimate(
            flops=flops, bytes_accessed=MIB, transcendentals=0
        ),
        compiler_params=pltpu.CompilerParams(vmem_limit_bytes=limit * MIB),
    )(*args)


def in_hbm(x):
    return pltpu.with_memory_space_constraint(x, pltpu.HBM)


def body(slabs, eps_occ, eps_vir):
    own = slabs[0]
    v, n = own.shape
    one = role_shift(own, 1)
    two = role_shift(own, -1)
    e_one = role_shift(eps_occ, 1)
    e_two = role_shift(eps_occ, -1)
    tile = (8, 128)
    s_one, s_two, s_own = (jnp.broadcast_to(e, tile) for e in (e_one, e_two, eps_occ))
    upper = jnp.broadcast_to(lax.axis_index("core").astype(F32), (8, v))
    pairs, oh, ol = call(
        prepare_kernel,
        ((v, v), (v, n), (v, n)),
        [],
        8,
        1 << 20,
        (eps_vir[None], own),
        [VMEM] * 2,
        (VMEM,) * 3,
    )
    piece = (16, 8, v)
    full = pltpu.VMEM((v, n), F32)
    keep, send, gift, later, near = call(
        pair_kernel,
        (piece, piece, (EARLY, n), (v - EARLY, n), (v, n)),
        [full] * 2 + [pltpu.VMEM((v, v), F32), pltpu.SemaphoreType.DMA((3,))],
        14,
        1 << 31,
        (upper, s_own, s_one, s_two, pairs, oh, ol, one, two),
        [VMEM] * 9,
        (VMEM, VMEM, HBM, HBM, HBM),
    )
    other = lax.ppermute(send, "core", [(0, 1), (1, 0)])
    gift = role_shift(gift, 1)
    later = role_shift(later, 1)
    parts = lax.all_to_all(
        keep + other, ("x", "far"), split_axis=0, concat_axis=0, tiled=True
    )
    (copies,) = call(fold_kernel, (piece,), [], 4, 1 << 20, (parts,), [VMEM], (VMEM,))
    copies = lax.all_to_all(
        copies, ("y", "near", "core"), split_axis=0, concat_axis=0, tiled=True
    )
    density = jnp.sum(copies.reshape(8, 16, v), axis=0)
    (grad,) = call(
        sum_kernel,
        ((v, n),),
        [full] * 2 + [pltpu.SemaphoreType.DMA((3, 3))],
        8,
        1 << 20,
        (in_hbm(near), gift, later),
        [HBM] * 3,
        (HBM,),
    )
    return grad[None], density


def solution(mesh):
    fine = Mesh(mesh.devices.reshape(FINE_SHAPE), FINE)
    placed = (P(FINE, None, None), P(FINE), P())
    return jax.shard_map(
        body,
        mesh=fine,
        in_specs=placed,
        out_specs=(P(FINE, None, None), P(("x", "far"), None)),
        check_vma=False,
    )
```

```python
import jax
import jax.numpy as jnp
from jax import lax
from jax.experimental import pallas as pl
from jax.experimental.pallas import tpu as pltpu
from jax.sharding import Mesh, PartitionSpec as P


FINE = ("y", "near", "core", "x", "far")
FINE_SHAPE = (4, 2, 2, 4, 4)
VMEM = pl.BlockSpec(memory_space=pltpu.VMEM)
SMEM = pl.BlockSpec(memory_space=pltpu.SMEM)
HBM = pl.BlockSpec(memory_space=pltpu.HBM)
F32, BF16 = jnp.float32, jnp.bfloat16
ROWS = ((1,), (1,))
PLAIN = ((1,), (0,))
MIB = 1 << 20
EARLY = 176


def role_shift(value, step):
    size = lax.axis_size("far")
    pairs = []
    for core, way in ((0, step), (1, -step)):
        base = core * size
        pairs += [(base + i, base + (i + way) % size) for i in range(size)]
    return lax.ppermute(value, ("core", "far"), pairs)


def split(x):
    high = x.astype(BF16)
    return high, (x - high.astype(F32)).astype(BF16)


def mm(a, b, contract):
    def dot(p, q):
        return lax.dot_general(p, q, (contract, ((), ())), preferred_element_type=F32)

    return dot(a[0], b[0]) + (dot(a[0], b[1]) + dot(a[1], b[0]))


def prepare_kernel(eps_vir, own, pairs, high, low):
    row = jnp.broadcast_to(eps_vir[...], pairs.shape)
    pairs[...] = row + row.T
    high[...], low[...] = split(own[...])


def spin(t):
    return split(2.0 * t - t.T)


def gift_kernel(e_one, e_two, pairs, one, two, *refs):
    gift, later, t_mid, ah, al, bh, bl, buf, sems = refs
    ah[...], al[...] = a = split(one[...])
    bh[...], bl[...] = b = split(two[...])
    t = mm(b, a, ROWS) / (e_one[0:1, 0:1] + e_two[0:1, 0:1] - pairs[...])
    buf[...] = mm(spin(t), a, PLAIN)
    out = [
        pltpu.make_async_copy(buf.at[:EARLY, :], gift, sems.at[0]),
        pltpu.make_async_copy(buf.at[EARLY:, :], later, sems.at[1]),
    ]
    for copy in out:
        copy.start()
    t_mid[...] = t
    for copy in out:
        copy.wait()


def density_kernel(upper, e_own, e_one, e_two, pairs, oh, ol, t_mid, *refs):
    ah, al, bh, bl, keep, send, near, total, dens, sem = refs
    o, a, b = (oh[...], ol[...]), (ah[...], al[...]), (bh[...], bl[...])
    mine, first, second = e_own[0:1, 0:1], e_one[0:1, 0:1], e_two[0:1, 0:1]
    t_one = mm(o, a, ROWS) / (mine + first - pairs[...])
    t_two = mm(o, b, ROWS) / (mine + second - pairs[...])
    s_one, s_two = spin(t_one), spin(t_two)
    total[...] = mm(s_one, a, PLAIN) + mm(s_two, b, PLAIN)
    out = pltpu.make_async_copy(total, near, sem)
    out.start()
    t = t_mid[...]
    dens[...] = (
        mm(split(t), spin(t), ROWS)
        + mm(split(t_one), s_one, ROWS)
        + mm(split(t_two), s_two, ROWS)
    )
    odd = upper[...] > 0.5
    for at in range(16):
        low = dens[at * 16 : at * 16 + 8, :]
        high = dens[at * 16 + 8 : at * 16 + 16, :]
        keep[at] = jnp.where(odd, high, low)
        send[at] = jnp.where(odd, low, high)
    out.wait()


def join_kernel(keep, other, copies):
    for at in range(keep.shape[0]):
        piece = keep[at] + other[at]
        copies[at // 4, 0, at % 4] = piece
        copies[at // 4, 1, at % 4] = piece


def sum_kernel(near, gift, later, grad, mine, other, sems):
    cuts = ((0, EARLY), (EARLY, EARLY + 40), (EARLY + 40, mine.shape[0]))
    copies = []
    for at, (low, high) in enumerate(cuts):
        rows = pl.ds(low, high - low)
        source = gift if at == 0 else later.at[pl.ds(low - EARLY, high - low), :]
        copies.append(
            (
                pltpu.make_async_copy(near.at[rows, :], mine.at[rows, :], sems.at[0, at]),
                pltpu.make_async_copy(source, other.at[rows, :], sems.at[1, at]),
                pltpu.make_async_copy(mine.at[rows, :], grad.at[rows, :], sems.at[2, at]),
            )
        )
        copies[-1][0].start()
        copies[-1][1].start()
    for at, (low, high) in enumerate(cuts):
        copies[at][0].wait()
        copies[at][1].wait()
        mine[low:high, :] = mine[low:high, :] + other[low:high, :]
        copies[at][2].start()
    for copy in copies:
        copy[2].wait()


def fold_kernel(pieces, copies):
    total = pieces[0]
    for at in range(1, pieces.shape[0]):
        total = total + pieces[at]
    total = total * (1.0 / 256.0)
    for at in range(copies.shape[0]):
        copies[at] = total


def call(kernel, out, scratch, limit, flops, args, in_specs, out_specs):
    return pl.pallas_call(
        kernel,
        out_shape=tuple(
            pltpu.HBM(s, F32)
            if spec is HBM
            else jax.ShapeDtypeStruct(s, BF16 if s == (256, 1024) else F32)
            for s, spec in zip(out, out_specs)
        ),
        in_specs=in_specs,
        out_specs=out_specs,
        scratch_shapes=scratch,
        cost_estimate=pl.CostEstimate(
            flops=flops, bytes_accessed=MIB, transcendentals=0
        ),
        compiler_params=pltpu.CompilerParams(vmem_limit_bytes=limit * MIB),
    )(*args)


def in_hbm(x):
    return pltpu.with_memory_space_constraint(x, pltpu.HBM)


def body(slabs, eps_occ, eps_vir):
    own = slabs[0]
    v, n = own.shape
    one = role_shift(own, 1)
    two = role_shift(own, -1)
    e_one = role_shift(eps_occ, 1)
    e_two = role_shift(eps_occ, -1)
    tile = (8, 128)
    s_one, s_two, s_own = (jnp.broadcast_to(e, tile) for e in (e_one, e_two, eps_occ))
    upper = jnp.broadcast_to(lax.axis_index("core").astype(F32), (8, v))
    pairs, oh, ol = call(
        prepare_kernel,
        ((v, v), (v, n), (v, n)),
        [],
        8,
        1 << 20,
        (eps_vir[None], own),
        [VMEM] * 2,
        (VMEM,) * 3,
    )
    piece = (16, 8, v)
    full = pltpu.VMEM((v, n), F32)
    gift, later, t_mid, *splits = call(
        gift_kernel,
        ((EARLY, n), (v - EARLY, n), (v, v)) + ((v, n),) * 4,
        [full, pltpu.SemaphoreType.DMA((2,))],
        12,
        1 << 31,
        (s_one, s_two, pairs, one, two),
        [VMEM] * 5,
        (HBM, HBM) + (VMEM,) * 5,
    )
    gift = role_shift(gift, 1)
    keep, send, near = call(
        density_kernel,
        (piece, piece, (v, n)),
        [full, pltpu.VMEM((v, v), F32), pltpu.SemaphoreType.DMA],
        12,
        1 << 31,
        (upper, s_own, s_one, s_two, pairs, oh, ol, t_mid, *splits),
        [VMEM] * 12,
        (VMEM, VMEM, HBM),
    )
    other = lax.ppermute(send, "core", [(0, 1), (1, 0)])
    later = role_shift(later, 1)
    (mine,) = call(
        join_kernel,
        ((4, 2, 4, 8, v),),
        [],
        4,
        1 << 20,
        (keep, other),
        [VMEM] * 2,
        (VMEM,),
    )
    parts = lax.all_to_all(
        mine.reshape(32, 8, v),
        ("x", "near", "far"),
        split_axis=0,
        concat_axis=0,
        tiled=True,
    )
    (copies,) = call(
        fold_kernel, ((8, 8, v),), [], 4, 1 << 20, (parts,), [VMEM], (VMEM,)
    )
    copies = lax.all_to_all(
        copies, ("y", "core"), split_axis=0, concat_axis=0, tiled=True
    )
    density = jnp.sum(copies.reshape(4, 16, v), axis=0)
    (grad,) = call(
        sum_kernel,
        ((v, n),),
        [full] * 2 + [pltpu.SemaphoreType.DMA((3, 3))],
        8,
        1 << 20,
        (in_hbm(near), gift, later),
        [HBM] * 3,
        (HBM,),
    )
    return grad[None], density


def solution(mesh):
    fine = Mesh(mesh.devices.reshape(FINE_SHAPE), FINE)
    placed = (P(FINE, None, None), P(FINE), P())
    return jax.shard_map(
        body,
        mesh=fine,
        in_specs=placed,
        out_specs=(P(FINE, None, None), P(("x", "far"), None)),
        check_vma=False,
    )
```

```python
import jax
import jax.numpy as jnp
from jax import lax
from jax.experimental import pallas as pl
from jax.experimental.pallas import tpu as pltpu
from jax.sharding import Mesh, PartitionSpec as P


FINE = ("y", "near", "core", "x", "far")
FINE_SHAPE = (4, 2, 2, 4, 4)
VMEM = pl.BlockSpec(memory_space=pltpu.VMEM)
SMEM = pl.BlockSpec(memory_space=pltpu.SMEM)
HBM = pl.BlockSpec(memory_space=pltpu.HBM)
F32, BF16 = jnp.float32, jnp.bfloat16
ROWS = ((1,), (1,))
PLAIN = ((1,), (0,))
MIB = 1 << 20
EARLY = 144


def role_shift(value, step):
    size = lax.axis_size("far")
    pairs = []
    for core, way in ((0, step), (1, -step)):
        base = core * size
        pairs += [(base + i, base + (i + way) % size) for i in range(size)]
    return lax.ppermute(value, ("core", "far"), pairs)


def split(x):
    high = x.astype(BF16)
    return high, (x - high.astype(F32)).astype(BF16)


def mm(a, b, contract):
    def dot(p, q):
        return lax.dot_general(p, q, (contract, ((), ())), preferred_element_type=F32)

    return dot(a[0], b[0]) + (dot(a[0], b[1]) + dot(a[1], b[0]))


def prepare_kernel(eps_vir, own, pairs, high, low):
    row = jnp.broadcast_to(eps_vir[...], pairs.shape)
    pairs[...] = row + row.T
    high[...], low[...] = split(own[...])


def spin(t):
    return split(2.0 * t - t.T)


def pair_kernel(upper, e_own, e_one, e_two, pairs, oh, ol, one, two, *refs):
    keep, send, gift, later, near, buf, total, dens, sems = refs
    o, a, b = (oh[...], ol[...]), split(one[...]), split(two[...])
    mine, first, second = e_own[0:1, 0:1], e_one[0:1, 0:1], e_two[0:1, 0:1]
    t = mm(b, a, ROWS) / (first + second - pairs[...])
    s = spin(t)
    buf[...] = mm(s, a, PLAIN)
    out = [
        pltpu.make_async_copy(buf.at[:EARLY, :], gift, sems.at[0]),
        pltpu.make_async_copy(buf.at[EARLY:, :], later, sems.at[2]),
    ]
    for copy in out:
        copy.start()
    t_one = mm(o, a, ROWS) / (mine + first - pairs[...])
    t_two = mm(o, b, ROWS) / (mine + second - pairs[...])
    s_one, s_two = spin(t_one), spin(t_two)
    total[...] = mm(s_one, a, PLAIN) + mm(s_two, b, PLAIN)
    out.append(pltpu.make_async_copy(total, near, sems.at[1]))
    out[2].start()
    dens[...] = (
        mm(split(t), s, ROWS)
        + mm(split(t_one), s_one, ROWS)
        + mm(split(t_two), s_two, ROWS)
    )
    odd = upper[...] > 0.5
    for at in range(16):
        low = dens[at * 16 : at * 16 + 8, :]
        high = dens[at * 16 + 8 : at * 16 + 16, :]
        keep[at] = jnp.where(odd, high, low)
        send[at] = jnp.where(odd, low, high)
    for copy in out:
        copy.wait()


def join_kernel(keep, other, copies):
    for at in range(keep.shape[0]):
        piece = keep[at] + other[at]
        copies[at // 4, 0, at % 4] = piece
        copies[at // 4, 1, at % 4] = piece


def sum_kernel(near, gift, later, grad, mine, other, sems):
    cuts = ((0, EARLY), (EARLY, EARLY + 56), (EARLY + 56, mine.shape[0]))
    copies = []
    for at, (low, high) in enumerate(cuts):
        rows = pl.ds(low, high - low)
        source = gift if at == 0 else later.at[pl.ds(low - EARLY, high - low), :]
        copies.append(
            (
                pltpu.make_async_copy(near.at[rows, :], mine.at[rows, :], sems.at[0, at]),
                pltpu.make_async_copy(source, other.at[rows, :], sems.at[1, at]),
                pltpu.make_async_copy(mine.at[rows, :], grad.at[rows, :], sems.at[2, at]),
            )
        )
        copies[-1][0].start()
        copies[-1][1].start()
    for at, (low, high) in enumerate(cuts):
        copies[at][0].wait()
        copies[at][1].wait()
        mine[low:high, :] = mine[low:high, :] + other[low:high, :]
        copies[at][2].start()
    for copy in copies:
        copy[2].wait()


def fold_kernel(pieces, copies):
    total = pieces[0]
    for at in range(1, pieces.shape[0]):
        total = total + pieces[at]
    total = total * (1.0 / 256.0)
    for at in range(copies.shape[0]):
        copies[at] = total


def call(kernel, out, scratch, limit, flops, args, in_specs, out_specs):
    return pl.pallas_call(
        kernel,
        out_shape=tuple(
            pltpu.HBM(s, F32)
            if spec is HBM
            else jax.ShapeDtypeStruct(s, BF16 if s == (256, 1024) else F32)
            for s, spec in zip(out, out_specs)
        ),
        in_specs=in_specs,
        out_specs=out_specs,
        scratch_shapes=scratch,
        cost_estimate=pl.CostEstimate(
            flops=flops, bytes_accessed=MIB, transcendentals=0
        ),
        compiler_params=pltpu.CompilerParams(vmem_limit_bytes=limit * MIB),
    )(*args)


def in_hbm(x):
    return pltpu.with_memory_space_constraint(x, pltpu.HBM)


def body(slabs, eps_occ, eps_vir):
    own = slabs[0]
    v, n = own.shape
    one = role_shift(own, 1)
    two = role_shift(own, -1)
    e_one = role_shift(eps_occ, 1)
    e_two = role_shift(eps_occ, -1)
    tile = (8, 128)
    s_one, s_two, s_own = (jnp.broadcast_to(e, tile) for e in (e_one, e_two, eps_occ))
    upper = jnp.broadcast_to(lax.axis_index("core").astype(F32), (8, v))
    pairs, oh, ol = call(
        prepare_kernel,
        ((v, v), (v, n), (v, n)),
        [],
        8,
        1 << 20,
        (eps_vir[None], own),
        [VMEM] * 2,
        (VMEM,) * 3,
    )
    piece = (16, 8, v)
    full = pltpu.VMEM((v, n), F32)
    keep, send, gift, later, near = call(
        pair_kernel,
        (piece, piece, (EARLY, n), (v - EARLY, n), (v, n)),
        [full] * 2 + [pltpu.VMEM((v, v), F32), pltpu.SemaphoreType.DMA((3,))],
        14,
        1 << 31,
        (upper, s_own, s_one, s_two, pairs, oh, ol, one, two),
        [VMEM] * 9,
        (VMEM, VMEM, HBM, HBM, HBM),
    )
    other = lax.ppermute(send, "core", [(0, 1), (1, 0)])
    gift = role_shift(gift, 1)
    later = role_shift(later, 1)
    (mine,) = call(
        join_kernel,
        ((4, 2, 4, 8, v),),
        [],
        4,
        1 << 20,
        (keep, other),
        [VMEM] * 2,
        (VMEM,),
    )
    parts = lax.all_to_all(
        mine.reshape(32, 8, v),
        ("x", "near", "far"),
        split_axis=0,
        concat_axis=0,
        tiled=True,
    )
    (copies,) = call(
        fold_kernel, ((8, 8, v),), [], 4, 1 << 20, (parts,), [VMEM], (VMEM,)
    )
    copies = lax.all_to_all(
        copies, ("y", "core"), split_axis=0, concat_axis=0, tiled=True
    )
    density = jnp.sum(copies.reshape(4, 16, v), axis=0)
    (grad,) = call(
        sum_kernel,
        ((v, n),),
        [full] * 2 + [pltpu.SemaphoreType.DMA((3, 3))],
        8,
        1 << 20,
        (in_hbm(near), gift, later),
        [HBM] * 3,
        (HBM,),
    )
    return grad[None], density


def solution(mesh):
    fine = Mesh(mesh.devices.reshape(FINE_SHAPE), FINE)
    placed = (P(FINE, None, None), P(FINE), P())
    return jax.shard_map(
        body,
        mesh=fine,
        in_specs=placed,
        out_specs=(P(FINE, None, None), P(("x", "far"), None)),
        check_vma=False,
    )
```

```python
import jax
import jax.numpy as jnp
from jax import lax
from jax.experimental import pallas as pl
from jax.experimental.pallas import tpu as pltpu
from jax.sharding import Mesh, PartitionSpec as P


FINE = ("y", "near", "core", "x", "far")
FINE_SHAPE = (4, 2, 2, 4, 4)
VMEM = pl.BlockSpec(memory_space=pltpu.VMEM)
SMEM = pl.BlockSpec(memory_space=pltpu.SMEM)
HBM = pl.BlockSpec(memory_space=pltpu.HBM)
F32, BF16 = jnp.float32, jnp.bfloat16
ROWS = ((1,), (1,))
PLAIN = ((1,), (0,))
MIB = 1 << 20


def role_shift(value, step):
    size = lax.axis_size("far")
    pairs = []
    for core, way in ((0, step), (1, -step)):
        base = core * size
        pairs += [(base + i, base + (i + way) % size) for i in range(size)]
    return lax.ppermute(value, ("core", "far"), pairs)


def split(x):
    high = x.astype(BF16)
    return high, (x - high.astype(F32)).astype(BF16)


def mm(a, b, contract):
    def dot(p, q):
        return lax.dot_general(p, q, (contract, ((), ())), preferred_element_type=F32)

    return dot(a[0], b[0]) + (dot(a[0], b[1]) + dot(a[1], b[0]))


def prepare_kernel(eps_vir, own, pairs, high, low):
    row = jnp.broadcast_to(eps_vir[...], pairs.shape)
    pairs[...] = row + row.T
    high[...], low[...] = split(own[...])


def spin(t):
    return split(2.0 * t - t.T)


def pair_kernel(upper, e_own, e_one, e_two, pairs, oh, ol, one, two, *refs):
    keep, send, gift, buf, dens, sem = refs
    o, a, b = (oh[...], ol[...]), split(one[...]), split(two[...])
    mine, first, second = e_own[0:1, 0:1], e_one[0:1, 0:1], e_two[0:1, 0:1]
    t = mm(b, a, ROWS) / (first + second - pairs[...])
    s = spin(t)
    buf[...] = mm(s, a, PLAIN)
    out = pltpu.make_async_copy(buf, gift, sem)
    out.start()
    t_one = mm(o, a, ROWS) / (mine + first - pairs[...])
    t_two = mm(o, b, ROWS) / (mine + second - pairs[...])
    s_one, s_two = spin(t_one), spin(t_two)
    dens[...] = (
        mm(split(t), s, ROWS)
        + mm(split(t_one), s_one, ROWS)
        + mm(split(t_two), s_two, ROWS)
    )
    odd = upper[...] > 0.5
    for at in range(16):
        low = dens[at * 16 : at * 16 + 8, :]
        high = dens[at * 16 + 8 : at * 16 + 16, :]
        keep[at] = jnp.where(odd, high, low)
        send[at] = jnp.where(odd, low, high)
    out.wait()


def near_kernel(e_own, e_one, e_two, pairs, oh, ol, one, two, near, total, sem):
    o, a, b = (oh[...], ol[...]), split(one[...]), split(two[...])
    mine, first, second = e_own[0:1, 0:1], e_one[0:1, 0:1], e_two[0:1, 0:1]
    s_one = spin(mm(o, a, ROWS) / (mine + first - pairs[...]))
    s_two = spin(mm(o, b, ROWS) / (mine + second - pairs[...]))
    total[...] = mm(s_one, a, PLAIN) + mm(s_two, b, PLAIN)
    out = pltpu.make_async_copy(total, near, sem)
    out.start()
    out.wait()


def join_kernel(keep, other, copies):
    for at in range(copies.shape[1]):
        piece = keep[at] + other[at]
        for copy in range(copies.shape[0]):
            copies[copy, at] = piece


def sum_kernel(near, gift, grad, mine, other, sems):
    parts = 4
    step = mine.shape[0] // parts
    copies = []
    for at in range(parts):
        rows = pl.ds(at * step, step)
        copies.append(
            (
                pltpu.make_async_copy(near.at[rows, :], mine.at[rows, :], sems.at[0, at]),
                pltpu.make_async_copy(gift.at[rows, :], other.at[rows, :], sems.at[1, at]),
                pltpu.make_async_copy(mine.at[rows, :], grad.at[rows, :], sems.at[2, at]),
            )
        )
        copies[-1][0].start()
        copies[-1][1].start()
    for at in range(parts):
        rows = slice(at * step, (at + 1) * step)
        copies[at][0].wait()
        copies[at][1].wait()
        mine[rows, :] = mine[rows, :] + other[rows, :]
        copies[at][2].start()
    for at in range(parts):
        copies[at][2].wait()


def fold_kernel(pieces, copies):
    total = pieces[0]
    for at in range(1, pieces.shape[0]):
        total = total + pieces[at]
    total = total * (1.0 / 256.0)
    for at in range(copies.shape[0]):
        row = at // 2 % 4 * 8
        copies[at] = total[row : row + 8, :]


def call(kernel, out, scratch, limit, flops, args, in_specs, out_specs):
    return pl.pallas_call(
        kernel,
        out_shape=tuple(
            pltpu.HBM(s, F32)
            if spec is HBM
            else jax.ShapeDtypeStruct(s, BF16 if s == (256, 1024) else F32)
            for s, spec in zip(out, out_specs)
        ),
        in_specs=in_specs,
        out_specs=out_specs,
        scratch_shapes=scratch,
        cost_estimate=pl.CostEstimate(
            flops=flops, bytes_accessed=MIB, transcendentals=0
        ),
        compiler_params=pltpu.CompilerParams(vmem_limit_bytes=limit * MIB),
    )(*args)


def in_hbm(x):
    return pltpu.with_memory_space_constraint(x, pltpu.HBM)


def body(slabs, eps_occ, eps_vir):
    own = slabs[0]
    v, n = own.shape
    one = role_shift(own, 1)
    two = role_shift(own, -1)
    e_one = role_shift(eps_occ, 1)
    e_two = role_shift(eps_occ, -1)
    tile = (8, 128)
    s_one, s_two, s_own = (jnp.broadcast_to(e, tile) for e in (e_one, e_two, eps_occ))
    upper = jnp.broadcast_to(lax.axis_index("core").astype(F32), (8, v))
    pairs, oh, ol = call(
        prepare_kernel,
        ((v, v), (v, n), (v, n)),
        [],
        8,
        1 << 20,
        (eps_vir[None], own),
        [VMEM] * 2,
        (VMEM,) * 3,
    )
    piece = (16, 8, v)
    full = pltpu.VMEM((v, n), F32)
    keep, send, gift = call(
        pair_kernel,
        (piece, piece, (v, n)),
        [full, pltpu.VMEM((v, v), F32), pltpu.SemaphoreType.DMA],
        14,
        1 << 31,
        (upper, s_own, s_one, s_two, pairs, oh, ol, one, two),
        [VMEM] * 9,
        (VMEM, VMEM, HBM),
    )
    other = lax.ppermute(send, "core", [(0, 1), (1, 0)])
    gift = role_shift(gift, 1)
    (mine,) = call(
        join_kernel, ((4,) + piece,), [], 4, 1 << 20, (keep, other), [VMEM] * 2, (VMEM,)
    )
    parts = lax.all_to_all(
        mine.reshape(16, 32, v), ("y", "x"), split_axis=0, concat_axis=0, tiled=True
    )
    (copies,) = call(fold_kernel, (piece,), [], 4, 1 << 20, (parts,), [VMEM], (VMEM,))
    copies = lax.all_to_all(
        copies, ("near", "far", "core"), split_axis=0, concat_axis=0, tiled=True
    )
    density = jnp.sum(copies.reshape(8, 16, v), axis=0)
    (near,) = call(
        near_kernel,
        ((v, n),),
        [full, pltpu.SemaphoreType.DMA],
        14,
        1 << 31,
        (s_own, s_one, s_two, pairs, oh, ol, one, two),
        [VMEM] * 8,
        (HBM,),
    )
    (grad,) = call(
        sum_kernel,
        ((v, n),),
        [full] * 2 + [pltpu.SemaphoreType.DMA((3, 4))],
        8,
        1 << 20,
        (in_hbm(near), gift),
        [HBM] * 2,
        (HBM,),
    )
    return grad[None], density


def solution(mesh):
    fine = Mesh(mesh.devices.reshape(FINE_SHAPE), FINE)
    placed = (P(FINE, None, None), P(FINE), P())
    return jax.shard_map(
        body,
        mesh=fine,
        in_specs=placed,
        out_specs=(P(FINE, None, None), P(("x", "far"), None)),
        check_vma=False,
    )
```

```python
import jax
import jax.numpy as jnp
from jax import lax
from jax.experimental import pallas as pl
from jax.experimental.pallas import tpu as pltpu
from jax.sharding import Mesh, PartitionSpec as P


FINE = ("y", "near", "core", "x", "far")
FINE_SHAPE = (4, 2, 2, 4, 4)
VMEM = pl.BlockSpec(memory_space=pltpu.VMEM)
SMEM = pl.BlockSpec(memory_space=pltpu.SMEM)
HBM = pl.BlockSpec(memory_space=pltpu.HBM)
F32, BF16 = jnp.float32, jnp.bfloat16
ROWS = ((1,), (1,))
PLAIN = ((1,), (0,))
MIB = 1 << 20


def role_shift(value, step):
    size = lax.axis_size("far")
    pairs = []
    for core, way in ((0, step), (1, -step)):
        base = core * size
        pairs += [(base + i, base + (i + way) % size) for i in range(size)]
    return lax.ppermute(value, ("core", "far"), pairs)


def split(x):
    high = x.astype(BF16)
    return high, (x - high.astype(F32)).astype(BF16)


def mm(a, b, contract):
    def dot(p, q):
        return lax.dot_general(p, q, (contract, ((), ())), preferred_element_type=F32)

    return dot(a[0], b[0]) + (dot(a[0], b[1]) + dot(a[1], b[0]))


def prepare_kernel(eps_vir, own, pairs, high, low, mask):
    row = lax.broadcasted_iota(jnp.int32, mask.shape, 0)
    mask[...] = jnp.where(row < 4, 1.0, 0.0)
    row = jnp.broadcast_to(eps_vir[...], pairs.shape)
    pairs[...] = row + row.T
    high[...], low[...] = split(own[...])


def spin(t):
    return split(2.0 * t - t.T)


def pair_kernel(upper, e_own, both, pairs, oh, ol, one, two, *refs):
    keep, send, gift, near, buf, total, dens, sems = refs
    o, a, b = (oh[...], ol[...]), split(one[...]), split(two[...])
    mine, first, second = e_own[0:1, 0:1], both[0:1, 0:1], both[4:5, 0:1]
    t = mm(b, a, ROWS) / (first + second - pairs[...])
    s = spin(t)
    buf[...] = mm(s, a, PLAIN)
    out = [pltpu.make_async_copy(buf, gift, sems.at[0])]
    out[0].start()
    t_one = mm(o, a, ROWS) / (mine + first - pairs[...])
    t_two = mm(o, b, ROWS) / (mine + second - pairs[...])
    s_one, s_two = spin(t_one), spin(t_two)
    total[...] = mm(s_one, a, PLAIN) + mm(s_two, b, PLAIN)
    out.append(pltpu.make_async_copy(total, near, sems.at[1]))
    out[1].start()
    dens[...] = (
        mm(split(t), s, ROWS)
        + mm(split(t_one), s_one, ROWS)
        + mm(split(t_two), s_two, ROWS)
    )
    odd = upper[...] > 0.5
    for at in range(16):
        low = dens[at * 16 : at * 16 + 8, :]
        high = dens[at * 16 + 8 : at * 16 + 16, :]
        keep[at] = jnp.where(odd, high, low)
        send[at] = jnp.where(odd, low, high)
    for copy in out:
        copy.wait()


def join_kernel(keep, other, copies):
    for at in range(copies.shape[1]):
        piece = keep[at] + other[at]
        for copy in range(copies.shape[0]):
            copies[copy, at] = piece


def sum_kernel(near, gift, grad, mine, other, sems):
    parts = 4
    step = mine.shape[0] // parts
    copies = []
    for at in range(parts):
        rows = pl.ds(at * step, step)
        copies.append(
            (
                pltpu.make_async_copy(near.at[rows, :], mine.at[rows, :], sems.at[0, at]),
                pltpu.make_async_copy(gift.at[rows, :], other.at[rows, :], sems.at[1, at]),
                pltpu.make_async_copy(mine.at[rows, :], grad.at[rows, :], sems.at[2, at]),
            )
        )
        copies[-1][0].start()
        copies[-1][1].start()
    for at in range(parts):
        rows = slice(at * step, (at + 1) * step)
        copies[at][0].wait()
        copies[at][1].wait()
        mine[rows, :] = mine[rows, :] + other[rows, :]
        copies[at][2].start()
    for at in range(parts):
        copies[at][2].wait()


def fold_kernel(pieces, copies):
    total = pieces[0]
    for at in range(1, pieces.shape[0]):
        total = total + pieces[at]
    total = total * (1.0 / 256.0)
    for at in range(copies.shape[0]):
        row = at // 2 % 4 * 8
        copies[at] = total[row : row + 8, :]


def call(kernel, out, scratch, limit, flops, args, in_specs, out_specs):
    return pl.pallas_call(
        kernel,
        out_shape=tuple(
            pltpu.HBM(s, F32)
            if spec is HBM
            else jax.ShapeDtypeStruct(s, BF16 if s == (256, 1024) else F32)
            for s, spec in zip(out, out_specs)
        ),
        in_specs=in_specs,
        out_specs=out_specs,
        scratch_shapes=scratch,
        cost_estimate=pl.CostEstimate(
            flops=flops, bytes_accessed=MIB, transcendentals=0
        ),
        compiler_params=pltpu.CompilerParams(vmem_limit_bytes=limit * MIB),
    )(*args)


def in_hbm(x):
    return pltpu.with_memory_space_constraint(x, pltpu.HBM)


def body(slabs, eps_occ, eps_vir):
    own = slabs[0]
    v, n = own.shape
    one = role_shift(own, 1)
    two = role_shift(own, -1)
    e_one = role_shift(eps_occ, 1)
    e_two = role_shift(eps_occ, -1)
    tile = (8, 128)
    s_own = jnp.broadcast_to(eps_occ, tile)
    upper = jnp.broadcast_to(lax.axis_index("core").astype(F32), (8, v))
    pairs, oh, ol, mask = call(
        prepare_kernel,
        ((v, v), (v, n), (v, n), (8, 128)),
        [],
        8,
        1 << 20,
        (eps_vir[None], own),
        [VMEM] * 2,
        (VMEM,) * 4,
    )
    both = e_one * mask + e_two * (1.0 - mask)
    piece = (16, 8, v)
    full = pltpu.VMEM((v, n), F32)
    keep, send, gift, near = call(
        pair_kernel,
        (piece, piece, (v, n), (v, n)),
        [full] * 2 + [pltpu.VMEM((v, v), F32), pltpu.SemaphoreType.DMA((2,))],
        14,
        1 << 31,
        (upper, s_own, both, pairs, oh, ol, one, two),
        [VMEM] * 8,
        (VMEM, VMEM, HBM, HBM),
    )
    other = lax.ppermute(send, "core", [(0, 1), (1, 0)])
    gift = role_shift(gift, 1)
    (mine,) = call(
        join_kernel, ((4,) + piece,), [], 4, 1 << 20, (keep, other), [VMEM] * 2, (VMEM,)
    )
    parts = lax.all_to_all(
        mine.reshape(16, 32, v), ("y", "x"), split_axis=0, concat_axis=0, tiled=True
    )
    (copies,) = call(fold_kernel, (piece,), [], 4, 1 << 20, (parts,), [VMEM], (VMEM,))
    copies = lax.all_to_all(
        copies, ("near", "far", "core"), split_axis=0, concat_axis=0, tiled=True
    )
    density = jnp.sum(copies.reshape(8, 16, v), axis=0)
    (grad,) = call(
        sum_kernel,
        ((v, n),),
        [full] * 2 + [pltpu.SemaphoreType.DMA((3, 4))],
        8,
        1 << 20,
        (in_hbm(near), gift),
        [HBM] * 2,
        (HBM,),
    )
    return grad[None], density


def solution(mesh):
    fine = Mesh(mesh.devices.reshape(FINE_SHAPE), FINE)
    placed = (P(FINE, None, None), P(FINE), P())
    return jax.shard_map(
        body,
        mesh=fine,
        in_specs=placed,
        out_specs=(P(FINE, None, None), P(("x", "far"), None)),
        check_vma=False,
    )
```

```python
import jax
import jax.numpy as jnp
from jax import lax
from jax.experimental import pallas as pl
from jax.experimental.pallas import tpu as pltpu
from jax.sharding import Mesh, PartitionSpec as P


FINE = ("y", "near", "core", "x", "far")
FINE_SHAPE = (4, 2, 2, 4, 4)
VMEM = pl.BlockSpec(memory_space=pltpu.VMEM)
SMEM = pl.BlockSpec(memory_space=pltpu.SMEM)
HBM = pl.BlockSpec(memory_space=pltpu.HBM)
F32, BF16 = jnp.float32, jnp.bfloat16
ROWS = ((1,), (1,))
PLAIN = ((1,), (0,))
MIB = 1 << 20
EARLY = 112


def role_shift(value, step):
    size = lax.axis_size("far")
    pairs = []
    for core, way in ((0, step), (1, -step)):
        base = core * size
        pairs += [(base + i, base + (i + way) % size) for i in range(size)]
    return lax.ppermute(value, ("core", "far"), pairs)


def split(x):
    high = x.astype(BF16)
    return high, (x - high.astype(F32)).astype(BF16)


def mm(a, b, contract):
    def dot(p, q):
        return lax.dot_general(p, q, (contract, ((), ())), preferred_element_type=F32)

    return dot(a[0], b[0]) + (dot(a[0], b[1]) + dot(a[1], b[0]))


def prepare_kernel(eps_vir, own, pairs, high, low):
    row = jnp.broadcast_to(eps_vir[...], pairs.shape)
    pairs[...] = row + row.T
    high[...], low[...] = split(own[...])


def spin(t):
    return split(2.0 * t - t.T)


def pair_kernel(upper, e_own, e_one, e_two, pairs, oh, ol, one, two, *refs):
    keep, send, gift, later, buf, dens, sems = refs
    o, a, b = (oh[...], ol[...]), split(one[...]), split(two[...])
    mine, first, second = e_own[0:1, 0:1], e_one[0:1, 0:1], e_two[0:1, 0:1]
    t = mm(b, a, ROWS) / (first + second - pairs[...])
    s = spin(t)
    buf[...] = mm(s, a, PLAIN)
    out = [
        pltpu.make_async_copy(buf.at[:EARLY, :], gift, sems.at[0]),
        pltpu.make_async_copy(buf.at[EARLY:, :], later, sems.at[1]),
    ]
    for copy in out:
        copy.start()
    t_one = mm(o, a, ROWS) / (mine + first - pairs[...])
    t_two = mm(o, b, ROWS) / (mine + second - pairs[...])
    s_one, s_two = spin(t_one), spin(t_two)
    dens[...] = (
        mm(split(t), s, ROWS)
        + mm(split(t_one), s_one, ROWS)
        + mm(split(t_two), s_two, ROWS)
    )
    odd = upper[...] > 0.5
    for at in range(16):
        low = dens[at * 16 : at * 16 + 8, :]
        high = dens[at * 16 + 8 : at * 16 + 16, :]
        keep[at] = jnp.where(odd, high, low)
        send[at] = jnp.where(odd, low, high)
    for copy in out:
        copy.wait()


def near_kernel(e_own, e_one, e_two, pairs, oh, ol, one, two, near, total, sem):
    o, a, b = (oh[...], ol[...]), split(one[...]), split(two[...])
    mine, first, second = e_own[0:1, 0:1], e_one[0:1, 0:1], e_two[0:1, 0:1]
    s_one = spin(mm(o, a, ROWS) / (mine + first - pairs[...]))
    s_two = spin(mm(o, b, ROWS) / (mine + second - pairs[...]))
    total[...] = mm(s_one, a, PLAIN) + mm(s_two, b, PLAIN)
    out = pltpu.make_async_copy(total, near, sem)
    out.start()
    out.wait()


def join_kernel(keep, other, copies):
    for at in range(keep.shape[0]):
        piece = keep[at] + other[at]
        copies[at // 4, 0, at % 4] = piece
        copies[at // 4, 1, at % 4] = piece


def sum_kernel(near, gift, later, grad, mine, other, sems):
    cuts = ((0, EARLY), (EARLY, EARLY + 72), (EARLY + 72, mine.shape[0]))
    copies = []
    for at, (low, high) in enumerate(cuts):
        rows = pl.ds(low, high - low)
        source = gift if at == 0 else later.at[pl.ds(low - EARLY, high - low), :]
        copies.append(
            (
                pltpu.make_async_copy(near.at[rows, :], mine.at[rows, :], sems.at[0, at]),
                pltpu.make_async_copy(source, other.at[rows, :], sems.at[1, at]),
                pltpu.make_async_copy(mine.at[rows, :], grad.at[rows, :], sems.at[2, at]),
            )
        )
        copies[-1][0].start()
        copies[-1][1].start()
    for at, (low, high) in enumerate(cuts):
        copies[at][0].wait()
        copies[at][1].wait()
        mine[low:high, :] = mine[low:high, :] + other[low:high, :]
        copies[at][2].start()
    for copy in copies:
        copy[2].wait()


def fold_kernel(pieces, copies):
    total = pieces[0]
    for at in range(1, pieces.shape[0]):
        total = total + pieces[at]
    total = total * (1.0 / 256.0)
    for at in range(copies.shape[0]):
        copies[at] = total


def call(kernel, out, scratch, limit, flops, args, in_specs, out_specs):
    return pl.pallas_call(
        kernel,
        out_shape=tuple(
            pltpu.HBM(s, F32)
            if spec is HBM
            else jax.ShapeDtypeStruct(s, BF16 if s == (256, 1024) else F32)
            for s, spec in zip(out, out_specs)
        ),
        in_specs=in_specs,
        out_specs=out_specs,
        scratch_shapes=scratch,
        cost_estimate=pl.CostEstimate(
            flops=flops, bytes_accessed=MIB, transcendentals=0
        ),
        compiler_params=pltpu.CompilerParams(vmem_limit_bytes=limit * MIB),
    )(*args)


def in_hbm(x):
    return pltpu.with_memory_space_constraint(x, pltpu.HBM)


def body(slabs, eps_occ, eps_vir):
    own = slabs[0]
    v, n = own.shape
    one = role_shift(own, 1)
    two = role_shift(own, -1)
    e_one = role_shift(eps_occ, 1)
    e_two = role_shift(eps_occ, -1)
    tile = (8, 128)
    s_one, s_two, s_own = (jnp.broadcast_to(e, tile) for e in (e_one, e_two, eps_occ))
    upper = jnp.broadcast_to(lax.axis_index("core").astype(F32), (8, v))
    pairs, oh, ol = call(
        prepare_kernel,
        ((v, v), (v, n), (v, n)),
        [],
        8,
        1 << 20,
        (eps_vir[None], own),
        [VMEM] * 2,
        (VMEM,) * 3,
    )
    piece = (16, 8, v)
    full = pltpu.VMEM((v, n), F32)
    keep, send, gift, later = call(
        pair_kernel,
        (piece, piece, (EARLY, n), (v - EARLY, n)),
        [full, pltpu.VMEM((v, v), F32), pltpu.SemaphoreType.DMA((2,))],
        14,
        1 << 31,
        (upper, s_own, s_one, s_two, pairs, oh, ol, one, two),
        [VMEM] * 9,
        (VMEM, VMEM, HBM, HBM),
    )
    other = lax.ppermute(send, "core", [(0, 1), (1, 0)])
    gift = role_shift(gift, 1)
    later = role_shift(later, 1)
    (mine,) = call(
        join_kernel,
        ((4, 2, 4, 8, v),),
        [],
        4,
        1 << 20,
        (keep, other),
        [VMEM] * 2,
        (VMEM,),
    )
    parts = lax.all_to_all(
        mine.reshape(32, 8, v),
        ("x", "near", "far"),
        split_axis=0,
        concat_axis=0,
        tiled=True,
    )
    (copies,) = call(
        fold_kernel, ((8, 8, v),), [], 4, 1 << 20, (parts,), [VMEM], (VMEM,)
    )
    copies = lax.all_to_all(
        copies, ("y", "core"), split_axis=0, concat_axis=0, tiled=True
    )
    density = jnp.sum(copies.reshape(4, 16, v), axis=0)
    (near,) = call(
        near_kernel,
        ((v, n),),
        [full, pltpu.SemaphoreType.DMA],
        14,
        1 << 31,
        (s_own, s_one, s_two, pairs, oh, ol, one, two),
        [VMEM] * 8,
        (HBM,),
    )
    (grad,) = call(
        sum_kernel,
        ((v, n),),
        [full] * 2 + [pltpu.SemaphoreType.DMA((3, 3))],
        8,
        1 << 20,
        (in_hbm(near), gift, later),
        [HBM] * 3,
        (HBM,),
    )
    return grad[None], density


def solution(mesh):
    fine = Mesh(mesh.devices.reshape(FINE_SHAPE), FINE)
    placed = (P(FINE, None, None), P(FINE), P())
    return jax.shard_map(
        body,
        mesh=fine,
        in_specs=placed,
        out_specs=(P(FINE, None, None), P(("x", "far"), None)),
        check_vma=False,
    )
```
